256 devices in a mesh: replica: 64 (over z_lo, y, x, core), tensor: 4 (over z_hi).
Axes of the slice: x: 4, y: 4, z: 8 (z_hi: 4, z_lo: 2; z = z_hi * 2 + z_lo), core: 2. Of those that a mesh axis runs over, the one named last changes fastest.
Arguments:
- x_in: bfloat16 [32768, 4096], P('replica', 'tensor'), may hold values from -6 to 6
- gate_z: bfloat16 [32768, 4096], P('replica', 'tensor'), may hold values from -6 to 6
- b_proj: bfloat16 [32768, 1024], P('replica', 'tensor'), may hold values from -2 to 2
- c_proj: bfloat16 [32768, 1024], P('replica', 'tensor'), may hold values from -2 to 2
- dt_raw: float32 [32768, 64], P('replica', 'tensor'), may hold values from -5 to 5
- a_log: float32 [64], P('tensor'), may hold values from 0 to 2.77
- dt_bias: float32 [64], P('tensor'), may hold values from -6 to -2
- skip_d: float32 [64], P('tensor'), may hold values from 0.5 to 1.5
- norm_gain: float32 [4096], P('tensor'), may hold values from 0.5 to 1.5
- out_weight: bfloat16 [64, 2048, 4096], P('replica', None, 'tensor'), may hold values from -0.25 to 0.25
- global_weight: float32 [2048, 4096], P('replica', 'tensor'), may hold values from -0.09375 to 0.09375
- momentum: float32 [2048, 4096], P('replica', 'tensor'), may hold values from -0.04 to 0.04
- target: bfloat16 [32768, 2048], P(('replica', 'tensor')), may hold values from -6 to 6
Outputs:
- grad_x: bfloat16 [32768, 4096], P('replica', 'tensor')
- new_weight: bfloat16 [2048, 4096], P(None, 'tensor')
- new_global: float32 [2048, 4096], P('replica', 'tensor')
- new_momentum: float32 [2048, 4096], P('replica', 'tensor')
The draws below stay inside these ranges and needn't reach their ends.
All inputs are finite; a program needn't handle non-finite values.
Results may differ from the reference program's by a relative error of at most 0.0085.
Values may be sent and summed in bfloat16 or wider, within the bound.
A program may use at most 128 MiB of HBM per device.

```python
import jax
import jax.numpy as jnp
from jax import lax

D = 2048
HEADS = 64
HEAD_DIM = 64
STATE = 128
GROUPS = 8
SPAN = 256
TOK = 512
INNER = 4096
REPLICAS = 64


def strengthened(drawn, stream_key, source, target, blocks, factor):
    def block_of(position):
        return (jnp.arange(drawn.shape[position]) // (drawn.shape[position] // blocks)).reshape((-1,) + (1,) * (drawn.ndim - 1 - position))

    one_side = jax.random.permutation(stream_key, blocks)[block_of(target)]
    second = (block_of(target) + blocks // 2) % blocks
    return jnp.where((block_of(source) == one_side) | (block_of(source) == second), factor * drawn, drawn)


def block_scale(own_key, shape, cuts, least, largest):
    loudness = 1.0
    for axis_at, shards_of in cuts:
        steps = jax.random.uniform(jax.random.fold_in(jax.random.fold_in(own_key, 6), axis_at), (shards_of,), jnp.float32, least / len(cuts), largest / len(cuts))
        loudness = loudness * jnp.repeat(jnp.exp(steps), shape[axis_at] // shards_of).reshape((-1,) + (1,) * (len(shape) - 1 - axis_at))
    return loudness


def scatter_about(stream_key, extent, deviation, most, cuts=(), held_as=jnp.bfloat16):
    values = jax.random.normal(stream_key, extent, jnp.float32) * deviation
    if len(cuts) > 0:
        values = block_scale(stream_key, extent, cuts, -0.22, 0.18) * values
    return jnp.clip(values, min=-most, max=most).astype(held_as)


def bell_draw_with(rng, extent, scale, reach, split, heavy, kind=jnp.bfloat16):
    drawn = scale * jax.random.normal(rng, extent, jnp.float32)
    if split:
        drawn = drawn * block_scale(rng, extent, split, -0.22, 0.18)
    return jnp.clip(strengthened(drawn, jax.random.fold_in(rng, 3), *heavy), -reach, reach).astype(kind)


def setup_inputs(seed: int = 0) -> dict:
    seeds = jax.random.split(jax.random.key(seed), 14)
    return {
        "x_in": scatter_about(seeds[0], (REPLICAS * TOK, INNER), 1.0, 6.0, ((0, 64), (1, 4))),
        "gate_z": scatter_about(seeds[1], (REPLICAS * TOK, INNER), 1.0, 6.0, ((0, 64), (1, 4))),
        "b_proj": scatter_about(seeds[2], (REPLICAS * TOK, GROUPS * STATE), 0.3, 2.0, ((0, 64), (1, 4))),
        "c_proj": scatter_about(seeds[3], (REPLICAS * TOK, GROUPS * STATE), 0.3, 2.0, ((0, 64), (1, 4))),
        "dt_raw": scatter_about(seeds[4], (REPLICAS * TOK, HEADS), 1.0, 5.0, ((0, 64), (1, 4)), jnp.float32),
        "a_log": jnp.clip(2.77 * jax.random.uniform(seeds[5], (HEADS,), jnp.float32) ** block_scale(seeds[5], (HEADS,), ((0, 4),), -0.2, 0.2), 0.0, 2.77),
        "dt_bias": jnp.clip(-6.0 + 4.0 * jax.random.uniform(seeds[6], (HEADS,), jnp.float32) ** block_scale(seeds[6], (HEADS,), ((0, 4),), -0.2, 0.2), -6.0, -2.0),
        "skip_d": jnp.clip(0.5 + 1.0 * jax.random.uniform(seeds[7], (HEADS,), jnp.float32) ** block_scale(seeds[7], (HEADS,), ((0, 4),), -0.2, 0.2), 0.5, 1.5),
        "norm_gain": jnp.clip(1.0 + 0.1 * jax.random.normal(seeds[8], (INNER,), jnp.float32), 0.5, 1.5),
        "out_weight": bell_draw_with(seeds[9], (REPLICAS, D, INNER), INNER ** -0.5, 0.25, ((0, 64), (2, 4)), (0, 1, 64, 4.0)),
        "global_weight": scatter_about(seeds[10], (D, INNER), INNER ** -0.5, 0.09375, ((0, 64), (1, 4)), jnp.float32),
        "momentum": scatter_about(seeds[11], (D, INNER), 0.005, 0.04, ((0, 64), (1, 4)), jnp.float32),
        "target": scatter_about(seeds[12], (REPLICAS * TOK, D), 1.0, 6.0, ((0, 256),)),
    }


inner_rate = 0.001
outer_rate = 0.7
outer_beta = 0.9
clip_rms = 0.005

def gated_ssd(inputs_f, gate_z, b_proj, c_proj, dt_raw, a_log, dt_bias, skip_d, norm_gain):
    tokens = inputs_f.shape[0]
    head_count = a_log.shape[0]
    group_count = b_proj.shape[1] // STATE
    per_group = head_count // group_count
    block_count = tokens // SPAN
    values = inputs_f.reshape(block_count, SPAN, group_count, per_group, HEAD_DIM)
    step_size = jax.nn.softplus(dt_raw.astype(jnp.float32) + dt_bias).reshape(block_count, SPAN, group_count, per_group)
    log_decay = (-jnp.exp(a_log)).reshape(group_count, per_group) * step_size
    cum_decay = jnp.cumsum(log_decay, axis=1)
    key_proj = b_proj.astype(jnp.float32).reshape(block_count, SPAN, group_count, STATE)
    query_proj = c_proj.astype(jnp.float32).reshape(block_count, SPAN, group_count, STATE)
    scores = jnp.einsum('clgn,csgn->cgls', query_proj, key_proj)
    cumulative = cum_decay.transpose(0, 2, 3, 1)
    gap_decay = cumulative[..., :, None] - cumulative[..., None, :]
    causal_mask = jnp.tril(jnp.ones((SPAN, SPAN), dtype=bool))
    decay_table = jnp.where(causal_mask, jnp.exp(jnp.where(causal_mask, gap_decay, 0.0)), 0.0)
    weights = scores[:, :, None] * decay_table * step_size.transpose(0, 2, 3, 1)[..., None, :]
    inside = jnp.einsum('cgrls,csgrp->clgrp', weights, values)
    tail_weight = jnp.exp(cum_decay[:, -1:] - cum_decay) * step_size
    states = jnp.einsum('csgn,csgr,csgrp->cgrpn', key_proj, tail_weight, values)
    span_fade = jnp.exp(cum_decay[:, -1])

    def carry_state(carried, inputs_pair):
        fade_now, state_now = inputs_pair
        return (fade_now[..., None, None] * carried + state_now, carried)
    _, entering = lax.scan(carry_state, jnp.zeros(states.shape[1:], jnp.float32), (span_fade, states))
    outside = jnp.einsum('clgn,cgrpn->clgrp', query_proj, entering) * jnp.exp(cum_decay)[..., None]
    ssd_out = inside + outside + skip_d.reshape(group_count, per_group)[..., None] * values
    width = per_group * HEAD_DIM
    gated_vals = ssd_out.reshape(tokens, group_count, width) * jax.nn.silu(gate_z.astype(jnp.float32)).reshape(tokens, group_count, width)
    inv_norm = lax.rsqrt(lax.optimization_barrier(jnp.mean(gated_vals * gated_vals, axis=-1, keepdims=True)) + 1e-05)
    return (gated_vals * inv_norm).reshape(tokens, head_count * HEAD_DIM) * norm_gain

def reference(x_in, gate_z, b_proj, c_proj, dt_raw, a_log, dt_bias, skip_d, norm_gain, out_weight, global_weight, momentum, target):
    replicas = out_weight.shape[0]
    width = x_in.shape[1]

    def per_replica(total_sum, pieces):
        x_rep, z_rep, b_rep, c_rep, dt_rep, w_rep, t_rep = pieces

        def forward(inputs_f):
            return gated_ssd(inputs_f, z_rep, b_rep, c_rep, dt_rep, a_log, dt_bias, skip_d, norm_gain)
        normed_f, pull_back = jax.vjp(forward, x_rep.astype(jnp.float32))
        normed = normed_f.astype(jnp.bfloat16)
        layer_out = lax.dot_general(normed, w_rep, (((1,), (1,)), ((), ())), preferred_element_type=jnp.float32)
        cotangent = (layer_out - t_rep.astype(jnp.float32)).astype(jnp.bfloat16)
        d_normed = jnp.dot(cotangent, w_rep, preferred_element_type=jnp.float32)
        weight_grad = lax.dot_general(cotangent, normed, (((0,), (0,)), ((), ())), preferred_element_type=jnp.float32)
        local_new = w_rep.astype(jnp.float32) - inner_rate * weight_grad
        grad_input = pull_back(d_normed)[0].astype(jnp.bfloat16)
        return (total_sum + local_new, grad_input)
    pieces = (x_in.reshape(replicas, TOK, width), gate_z.reshape(replicas, TOK, width), b_proj.reshape(replicas, TOK, -1), c_proj.reshape(replicas, TOK, -1), dt_raw.reshape(replicas, TOK, -1), out_weight, target.reshape(replicas, TOK, -1))
    total_sum, grads = lax.scan(per_replica, jnp.zeros(out_weight.shape[1:], jnp.float32), pieces)
    grad_x = grads.reshape(replicas * TOK, width)
    delta = global_weight - total_sum / replicas
    factor = jnp.minimum(1.0, clip_rms / jnp.sqrt(jnp.mean(delta * delta) + 1e-06))
    clipped = factor * delta
    new_momentum = outer_beta * momentum + clipped
    new_global = global_weight - outer_rate * (clipped + outer_beta * new_momentum)
    return (grad_x, new_global.astype(jnp.bfloat16), new_global, new_momentum)
```

```python
import jax
import jax.numpy as jnp
from jax import lax
from jax.experimental import pallas as pl
from jax.experimental.pallas import tpu as pltpu
from jax.sharding import Mesh
from jax.sharding import PartitionSpec as P

HEAD_DIM = 64
STATE = 128
SPAN = 256
REPLICA = ("replica_0", "replica_1", "replica_2", "replica_3")
REPLICA_TENSOR = ("replica_0", "replica_1", "replica_2", "replica_3", "tensor")


inner_rate = 0.001
outer_rate = 0.7
outer_beta = 0.9
clip_rms = 0.005
MESH = pl.DeviceIdType.MESH
UNITS = 8
FEATURES = 256
TOKENS = 128
WIDTH = 1024
ENTRIES = 2048 * 4096
KINDS = ("far", "near", "mid", "ahead", "behind", "relay")
LAGS = (0, 3, 4, 5, 6, 7, 8)


def exchange_kernel(
    normed,
    weight,
    target,
    global_own,
    momentum_own,
    d_normed,
    full,
    new_global,
    new_momentum,
    part,
    s_far,
    s_near,
    s_mid,
    r_far,
    r_near,
    r_mid,
    cot,
    fresh,
    r_core,
    s_core,
    r_x,
    s_x,
    r_y,
    s_y,
    s_z,
    r_z,
    sq_a,
    sq_b,
    sq_c,
    z_send,
    z_recv,
    core_send,
    core_recv,
    x_send,
    x_recv,
    y_send,
    y_recv,
    zl_send,
    zl_recv,
    a_send,
    a_recv,
    b_send,
    b_recv,
    c_send,
    c_recv,
    g_send,
    g_recv,
):
    zl = lax.axis_index("replica_0")
    y = lax.axis_index("replica_1")
    x = lax.axis_index("replica_2")
    c = lax.axis_index("replica_3")
    j = lax.axis_index("tensor")

    def on_z(kz, kj):
        return {"replica_0": lax.rem(zl + kz, 2), "tensor": lax.rem(j + kj, 4)}

    def on_x(kx, kc):
        return {"replica_2": lax.rem(x + kx, 4), "replica_3": lax.rem(c + kc, 2)}

    def on_y(ky):
        return {"replica_1": lax.rem(y + ky, 4)}

    z_peers = [(kz, kj) for kz in range(2) for kj in range(4) if kz + kj]
    x_peers = [(kx, kc) for kx in range(4) for kc in range(2) if kx + kc]
    barrier = pltpu.get_barrier_semaphore()
    for kz, kj in z_peers:
        pl.semaphore_signal(barrier, inc=1, device_id=on_z(kz, kj), device_id_type=MESH)
    for kx, kc in x_peers:
        pl.semaphore_signal(barrier, inc=1, device_id=on_x(kx, kc), device_id_type=MESH)
    for ky in range(1, 4):
        pl.semaphore_signal(barrier, inc=1, device_id=on_y(ky), device_id_type=MESH)
    pl.semaphore_wait(barrier, len(z_peers) + len(x_peers) + 3)

    def remote(src, dst, send_sem, recv_sem, device):
        return pltpu.make_async_remote_copy(
            src_ref=src,
            dst_ref=dst,
            send_sem=send_sem,
            recv_sem=recv_sem,
            device_id=device,
            device_id_type=MESH,
        )

    def way(u):
        return 1 - 2 * lax.rem(u, 2)

    def shard(step):
        return lax.rem(j + step + 4, 4)

    def z_copy(kind, u):
        d = way(u)
        ahead = {"tensor": shard(d)}
        behind = {"tensor": shard(-d)}
        src, dst, device = {
            "far": lambda: (s_far.at[u], r_far.at[u], behind),
            "near": lambda: (s_near.at[u], r_near.at[u], ahead),
            "mid": lambda: (s_mid.at[u], r_mid.at[u], behind),
            "ahead": lambda: (cot.at[u, j], cot.at[u, j], ahead),
            "behind": lambda: (cot.at[u, j], cot.at[u, j], behind),
            "relay": lambda: (cot.at[u, shard(-d)], cot.at[u, shard(-d)], ahead),
        }[kind]()
        slot = KINDS.index(kind)
        return remote(src, dst, z_send.at[u, slot], z_recv.at[u, slot], device)

    def core_copy(u):
        return remote(
            fresh.at[u, :, 1 - c],
            r_core.at[u],
            core_send.at[u],
            core_recv.at[u],
            {"replica_3": 1 - c},
        )

    def x_copy(u, k):
        there = lax.rem(x + k, 4)
        return remote(
            s_core.at[u, there],
            r_x.at[u, k - 1],
            x_send.at[u, k - 1],
            x_recv.at[u, k - 1],
            {"replica_2": there},
        )

    def y_copy(half, k):
        there = lax.rem(y + k, 4)
        return remote(
            s_x.at[half * 4 + there],
            r_y.at[half, k - 1],
            y_send.at[half, k - 1],
            y_recv.at[half, k - 1],
            {"replica_1": there},
        )

    def rows_of(u):
        return pl.ds(pl.multiple_of(u * FEATURES, FEATURES), FEATURES)

    def begin(u):
        d = way(u)
        products = lax.dot_general(
            normed[...],
            weight[rows_of(u), :],
            (((1,), (1,)), ((), ())),
            preferred_element_type=jnp.float32,
        )
        part[u] = products.reshape(4, TOKENS, FEATURES)
        s_far[u] = part[u, shard(2)].astype(jnp.bfloat16)
        s_near[u] = part[u, shard(d)].astype(jnp.bfloat16)
        z_copy("far", u).start()
        z_copy("near", u).start()

    def pass_on(u):
        z_copy("far", u).wait_recv()
        s_mid[u] = (r_far[u].astype(jnp.float32) + part[u, shard(-way(u))]).astype(jnp.bfloat16)
        z_copy("mid", u).start()

    def own(u):
        z_copy("near", u).wait_recv()
        z_copy("mid", u).wait_recv()
        total = part[u, j] + r_near[u].astype(jnp.float32) + r_mid[u].astype(jnp.float32)
        cot[u, j] = (total - target[:, rows_of(u)].astype(jnp.float32)).astype(jnp.bfloat16)
        z_copy("ahead", u).start()
        z_copy("behind", u).start()

    def relay(u):
        z_copy("ahead", u).wait_recv()
        z_copy("relay", u).start()

    def gradients(u):
        z_copy("behind", u).wait_recv()
        z_copy("relay", u).wait_recv()
        whole = cot[u].reshape(4 * TOKENS, FEATURES)
        for first in range(0, WIDTH, 512):
            cols = slice(first, first + 512)
            rows = weight[rows_of(u), cols]
            grad = lax.dot_general(
                whole,
                normed[:, cols],
                (((0,), (0,)), ((), ())),
                preferred_element_type=jnp.float32,
            )
            moved = (rows.astype(jnp.float32) - inner_rate * grad).astype(jnp.bfloat16)
            fresh[u, :, :, :, cols] = moved.reshape(4, 2, 32, 512)
            d_normed[:, cols] += jnp.dot(whole, rows, preferred_element_type=jnp.float32)
        core_copy(u).start()

    def over_x(u):
        core_copy(u).wait_recv()
        for i in range(4):
            both = fresh[u, i, c].astype(jnp.float32) + r_core[u, i].astype(jnp.float32)
            s_core[u, i] = both.astype(jnp.bfloat16)
        for k in range(1, 4):
            x_copy(u, k).start()

    def after_x(u):
        total = s_core[u, x].astype(jnp.float32)
        for k in range(1, 4):
            x_copy(u, k).wait_recv()
            total = total + r_x[u, k - 1].astype(jnp.float32)
        s_x[u] = total.astype(jnp.bfloat16)

    d_normed[...] = jnp.zeros_like(d_normed)
    stages = list(zip((begin, pass_on, own, relay, gradients, over_x, after_x), LAGS))

    @pl.loop(0, UNITS + LAGS[-1])
    def _(k):
        for stage, lag in stages:

            @pl.when((k >= lag) & (k < UNITS + lag))
            def _():
                stage(k - lag)

    for half in range(2):
        for k in range(1, 4):
            y_copy(half, k).start()
    for half in range(2):
        total = s_x[half * 4 + y].astype(jnp.float32)
        for k in range(1, 4):
            y_copy(half, k).wait_recv()
            total = total + r_y[half, k - 1].astype(jnp.float32)
        s_y[half] = total
    s_z[...] = s_y[1 - zl].astype(jnp.bfloat16)
    over_z = remote(s_z, r_z, zl_send.at[0], zl_recv.at[0], on_z(1, 0))
    over_z.start()
    over_z.wait_recv()
    delta = global_own[...] - (s_y[zl] + r_z[...].astype(jnp.float32)) * (1.0 / 64)

    squares = jnp.sum((delta * delta).reshape(4, 8, WIDTH), axis=0)
    folded = squares[:, :128]
    for first in range(128, WIDTH, 128):
        folded = folded + squares[:, first : first + 128]
    sq_a[x, c] = folded
    a_copies = [
        remote(sq_a.at[x, c], sq_a.at[x, c], a_send.at[i], a_recv.at[i], on_x(*peer))
        for i, peer in enumerate(x_peers)
    ]
    for copy in a_copies:
        copy.start()
    for copy in a_copies:
        copy.wait_recv()
    sq_b[y] = jnp.sum(sq_a[...].reshape(8, 8, 128), axis=0)
    b_copies = [
        remote(sq_b.at[y], sq_b.at[y], b_send.at[k - 1], b_recv.at[k - 1], on_y(k))
        for k in range(1, 4)
    ]
    for copy in b_copies:
        copy.start()
    for copy in b_copies:
        copy.wait_recv()
    sq_c[zl, j] = jnp.sum(sq_b[...], axis=0)
    c_copies = [
        remote(sq_c.at[zl, j], sq_c.at[zl, j], c_send.at[i], c_recv.at[i], on_z(*peer))
        for i, peer in enumerate(z_peers)
    ]
    for copy in c_copies:
        copy.start()
    for copy in c_copies:
        copy.wait_recv()
    square_sum = jnp.sum(jnp.sum(sq_c[...].reshape(8, 8, 128), axis=0), keepdims=True)
    factor = jnp.minimum(1.0, clip_rms / jnp.sqrt(square_sum / ENTRIES + 1e-06))
    clipped = factor * delta
    moment = outer_beta * momentum_own[...] + clipped
    moved = global_own[...] - outer_rate * (clipped + outer_beta * moment)
    new_momentum[...] = moment
    new_global[...] = moved
    full[zl, y, x, c] = moved.astype(jnp.bfloat16)

    def gather(index, src, device):
        return remote(src, src, g_send.at[index], g_recv.at[index], device)

    mine = full.at[zl, y, x, c]
    first = gather(0, mine, on_z(1, 0))
    first.start()
    first.wait_recv()
    left, right = pl.ds(0, WIDTH // 2), pl.ds(WIDTH // 2, WIDTH // 2)
    near = [gather(k, full.at[:, y, x, c, :, left], on_y(k)) for k in range(1, 4)]
    near += [gather(3 + k, full.at[:, y, x, c, :, right], on_x(k, 0)) for k in range(1, 4)]
    for copy in near:
        copy.start()
    for copy in near:
        copy.wait_recv()
    far = [gather(6 + k, full.at[:, :, x, c, :, left], on_x(k, 0)) for k in range(1, 4)]
    far += [gather(9 + k, full.at[:, y, :, c, :, right], on_y(k)) for k in range(1, 4)]
    for i in (0, 3, 2, 5, 1, 4):
        far[i].start()

    def to_core(index, k):
        if index < 4:
            src = full.at[:, :, lax.rem(x + 4 - k, 4), c, :, left]
        else:
            src = full.at[:, lax.rem(y + 4 - k, 4), :, c, :, right]
        return gather(13 + index, src, on_x(0, 1))

    across = [to_core(0, 0), to_core(4, 0)]
    for copy in across:
        copy.start()
    for k in (1, 3, 2):
        for base in (0, 3):
            far[base + k - 1].wait_recv()
            copy = to_core(k if base == 0 else 4 + k, k)
            copy.start()
            across.append(copy)
    for copy in across:
        copy.wait_recv()

    for copy in [over_z, first, *a_copies, *b_copies, *c_copies, *near, *far, *across]:
        copy.wait_send()
    for half in range(2):
        for k in range(1, 4):
            y_copy(half, k).wait_send()

    @pl.loop(0, UNITS)
    def _(u):
        for kind in KINDS:
            z_copy(kind, u).wait_send()
        core_copy(u).wait_send()
        for k in range(1, 4):
            x_copy(u, k).wait_send()


def exchange(normed, weight, target, global_own, momentum_own):
    half = jnp.bfloat16
    piece = (UNITS, TOKENS, FEATURES)
    dma = pltpu.SemaphoreType.DMA
    vmem = pl.BlockSpec(memory_space=pltpu.VMEM)
    d_normed, full, new_global, new_momentum = pl.pallas_call(
        exchange_kernel,
        out_shape=(
            jax.ShapeDtypeStruct((4 * TOKENS, WIDTH), jnp.float32),
            jax.ShapeDtypeStruct((2, 4, 4, 2, 32, WIDTH), half),
            jax.ShapeDtypeStruct((32, WIDTH), jnp.float32),
            jax.ShapeDtypeStruct((32, WIDTH), jnp.float32),
        ),
        in_specs=[vmem] * 5,
        out_specs=[vmem] * 4,
        scratch_shapes=[
            pltpu.VMEM((UNITS, 4, TOKENS, FEATURES), jnp.float32),
            *[pltpu.VMEM(piece, half)] * 6,
            pltpu.VMEM((UNITS, 4, TOKENS, FEATURES), half),
            pltpu.VMEM((UNITS, 4, 2, 32, WIDTH), half),
            pltpu.VMEM((UNITS, 4, 32, WIDTH), half),
            pltpu.VMEM((UNITS, 4, 32, WIDTH), half),
            pltpu.VMEM((UNITS, 3, 32, WIDTH), half),
            pltpu.VMEM((UNITS, 32, WIDTH), half),
            pltpu.VMEM((2, 3, 32, WIDTH), half),
            pltpu.VMEM((2, 32, WIDTH), jnp.float32),
            pltpu.VMEM((32, WIDTH), half),
            pltpu.VMEM((32, WIDTH), half),
            pltpu.VMEM((4, 2, 8, 128), jnp.float32),
            pltpu.VMEM((4, 8, 128), jnp.float32),
            pltpu.VMEM((2, 4, 8, 128), jnp.float32),
            *[dma((UNITS, len(KINDS)))] * 2,
            *[dma((UNITS,))] * 2,
            *[dma((UNITS, 3))] * 2,
            *[dma((2, 3))] * 2,
            *[dma((1,))] * 2,
            *[dma((7,))] * 2,
            *[dma((3,))] * 2,
            *[dma((7,))] * 2,
            *[dma((21,))] * 2,
        ],
        compiler_params=pltpu.CompilerParams(
            collective_id=0, has_side_effects=True, vmem_limit_bytes=60 * 2**20
        ),
    )(normed, weight, target, global_own, momentum_own)
    return d_normed, full.reshape(2048, WIDTH), new_global, new_momentum


def gated_ssd(inputs_f, gate_z, b_proj, c_proj, dt_raw, a_log, dt_bias, skip_d, norm_gain):
    tokens = inputs_f.shape[0]
    head_count = a_log.shape[0]
    group_count = b_proj.shape[1] // STATE
    per_group = head_count // group_count
    block_count = tokens // SPAN
    values = inputs_f.reshape(block_count, SPAN, group_count, per_group, HEAD_DIM)
    step_size = jax.nn.softplus(dt_raw + dt_bias).reshape(block_count, SPAN, group_count, per_group)
    log_decay = (-jnp.exp(a_log)).reshape(group_count, per_group) * step_size
    cum_decay = jnp.cumsum(log_decay, axis=1)
    key_proj = b_proj.astype(jnp.float32).reshape(block_count, SPAN, group_count, STATE)
    query_proj = c_proj.astype(jnp.float32).reshape(block_count, SPAN, group_count, STATE)
    scores = jnp.einsum("clgn,csgn->cgls", query_proj, key_proj)
    cumulative = cum_decay.transpose(0, 2, 3, 1)
    gap_decay = cumulative[..., :, None] - cumulative[..., None, :]
    causal_mask = jnp.tril(jnp.ones((SPAN, SPAN), dtype=bool))
    decay_table = jnp.where(causal_mask, jnp.exp(jnp.where(causal_mask, gap_decay, 0.0)), 0.0)
    weights = scores[:, :, None] * decay_table * step_size.transpose(0, 2, 3, 1)[..., None, :]
    inside = jnp.einsum("cgrls,csgrp->clgrp", weights, values)
    tail_weight = jnp.exp(cum_decay[:, -1:] - cum_decay) * step_size
    states = jnp.einsum("csgn,csgr,csgrp->cgrpn", key_proj, tail_weight, values)
    span_fade = jnp.exp(cum_decay[:, -1])

    def carry_state(carried, inputs_pair):
        fade_now, state_now = inputs_pair
        return (fade_now[..., None, None] * carried + state_now, carried)

    _, entering = lax.scan(
        carry_state, jnp.zeros(states.shape[1:], jnp.float32), (span_fade, states)
    )
    outside = jnp.einsum("clgn,cgrpn->clgrp", query_proj, entering) * jnp.exp(cum_decay)[..., None]
    ssd_out = inside + outside + skip_d.reshape(group_count, per_group)[..., None] * values
    width = per_group * HEAD_DIM
    gated_vals = ssd_out.reshape(tokens, group_count, width) * jax.nn.silu(
        gate_z.astype(jnp.float32)
    ).reshape(tokens, group_count, width)
    inv_norm = lax.rsqrt(jnp.mean(gated_vals * gated_vals, axis=-1, keepdims=True) + 1e-05)
    return (gated_vals * inv_norm).reshape(tokens, head_count * HEAD_DIM) * norm_gain


def shards(
    x_in,
    gate_z,
    b_proj,
    c_proj,
    dt_raw,
    a_log,
    dt_bias,
    skip_d,
    norm_gain,
    out_weight,
    global_weight,
    momentum,
    target,
):
    local_weight = out_weight[0]

    def forward(inputs_f):
        return gated_ssd(
            inputs_f, gate_z, b_proj, c_proj, dt_raw, a_log, dt_bias, skip_d, norm_gain
        )

    normed_f, pull_back = jax.vjp(forward, x_in.astype(jnp.float32))
    normed = normed_f.astype(jnp.bfloat16)
    d_normed, new_weight, new_global, new_momentum = exchange(
        normed, local_weight, target, global_weight, momentum
    )
    grad_input = pull_back(d_normed)[0]
    return (grad_input.astype(jnp.bfloat16), new_weight, new_global, new_momentum)


def solution(mesh):
    torus = Mesh(
        mesh.devices.reshape(2, 4, 4, 2, mesh.shape["tensor"]),
        ("replica_0", "replica_1", "replica_2", "replica_3", "tensor"),
    )
    in_specs = (
        P(REPLICA, "tensor"),
        P(REPLICA, "tensor"),
        P(REPLICA, "tensor"),
        P(REPLICA, "tensor"),
        P(REPLICA, "tensor"),
        P("tensor"),
        P("tensor"),
        P("tensor"),
        P("tensor"),
        P(REPLICA, None, "tensor"),
        P(REPLICA, "tensor"),
        P(REPLICA, "tensor"),
        P(REPLICA_TENSOR, None),
    )
    out_specs = (
        P(REPLICA, "tensor"),
        P(None, "tensor"),
        P(REPLICA, "tensor"),
        P(REPLICA, "tensor"),
    )
    return jax.shard_map(
        shards, mesh=torus, in_specs=in_specs, out_specs=out_specs, check_vma=False
    )
```

```python
import jax
import jax.numpy as jnp
from jax import lax
from jax.experimental import pallas as pl
from jax.experimental.pallas import tpu as pltpu
from jax.sharding import Mesh
from jax.sharding import PartitionSpec as P

HEAD_DIM = 64
STATE = 128
SPAN = 256
REPLICA = ("replica_0", "replica_1", "replica_2", "replica_3")
REPLICA_TENSOR = ("replica_0", "replica_1", "replica_2", "replica_3", "tensor")


inner_rate = 0.001
outer_rate = 0.7
outer_beta = 0.9
clip_rms = 0.005
MESH = pl.DeviceIdType.MESH
UNITS = 8
FEATURES = 256
TOKENS = 128
WIDTH = 1024
ENTRIES = 2048 * 4096
KINDS = ("far", "near", "mid", "ahead", "behind", "relay")
LAGS = (0, 3, 4, 5, 6, 7, 8)


def exchange_kernel(
    normed,
    weight,
    target,
    global_own,
    momentum_own,
    d_normed,
    full,
    new_global,
    new_momentum,
    part,
    s_far,
    s_near,
    s_mid,
    r_far,
    r_near,
    r_mid,
    cot,
    fresh,
    r_core,
    s_core,
    r_x,
    s_x,
    r_y,
    s_y,
    s_z,
    r_z,
    sq_a,
    sq_b,
    sq_c,
    z_send,
    z_recv,
    core_send,
    core_recv,
    x_send,
    x_recv,
    y_send,
    y_recv,
    zl_send,
    zl_recv,
    a_send,
    a_recv,
    b_send,
    b_recv,
    c_send,
    c_recv,
    g_send,
    g_recv,
):
    zl = lax.axis_index("replica_0")
    y = lax.axis_index("replica_1")
    x = lax.axis_index("replica_2")
    c = lax.axis_index("replica_3")
    j = lax.axis_index("tensor")

    def on_z(kz, kj):
        return {"replica_0": lax.rem(zl + kz, 2), "tensor": lax.rem(j + kj, 4)}

    def on_x(kx, kc):
        return {"replica_2": lax.rem(x + kx, 4), "replica_3": lax.rem(c + kc, 2)}

    def on_y(ky):
        return {"replica_1": lax.rem(y + ky, 4)}

    z_peers = [(kz, kj) for kz in range(2) for kj in range(4) if kz + kj]
    x_peers = [(kx, kc) for kx in range(4) for kc in range(2) if kx + kc]
    barrier = pltpu.get_barrier_semaphore()
    for kz, kj in z_peers:
        pl.semaphore_signal(barrier, inc=1, device_id=on_z(kz, kj), device_id_type=MESH)
    for kx, kc in x_peers:
        pl.semaphore_signal(barrier, inc=1, device_id=on_x(kx, kc), device_id_type=MESH)
    for ky in range(1, 4):
        pl.semaphore_signal(barrier, inc=1, device_id=on_y(ky), device_id_type=MESH)
    pl.semaphore_wait(barrier, len(z_peers) + len(x_peers) + 3)

    def remote(src, dst, send_sem, recv_sem, device):
        return pltpu.make_async_remote_copy(
            src_ref=src,
            dst_ref=dst,
            send_sem=send_sem,
            recv_sem=recv_sem,
            device_id=device,
            device_id_type=MESH,
        )

    def way(u):
        return 1 - 2 * lax.rem(u, 2)

    def shard(step):
        return lax.rem(j + step + 4, 4)

    def z_copy(kind, u):
        d = way(u)
        ahead = {"tensor": shard(d)}
        behind = {"tensor": shard(-d)}
        src, dst, device = {
            "far": lambda: (s_far.at[u], r_far.at[u], behind),
            "near": lambda: (s_near.at[u], r_near.at[u], ahead),
            "mid": lambda: (s_mid.at[u], r_mid.at[u], behind),
            "ahead": lambda: (cot.at[u, j], cot.at[u, j], ahead),
            "behind": lambda: (cot.at[u, j], cot.at[u, j], behind),
            "relay": lambda: (cot.at[u, shard(-d)], cot.at[u, shard(-d)], ahead),
        }[kind]()
        slot = KINDS.index(kind)
        return remote(src, dst, z_send.at[u, slot], z_recv.at[u, slot], device)

    def core_copy(u):
        return remote(
            fresh.at[u, :, 1 - c],
            r_core.at[u],
            core_send.at[u],
            core_recv.at[u],
            {"replica_3": 1 - c},
        )

    def x_copy(u, k):
        there = lax.rem(x + k, 4)
        return remote(
            s_core.at[u, there],
            r_x.at[u, k - 1],
            x_send.at[u, k - 1],
            x_recv.at[u, k - 1],
            {"replica_2": there},
        )

    def y_copy(half, k):
        there = lax.rem(y + k, 4)
        return remote(
            s_x.at[half * 4 + there],
            r_y.at[half, k - 1],
            y_send.at[half, k - 1],
            y_recv.at[half, k - 1],
            {"replica_1": there},
        )

    def rows_of(u):
        return pl.ds(pl.multiple_of(u * FEATURES, FEATURES), FEATURES)

    def begin(u):
        d = way(u)
        products = lax.dot_general(
            normed[...],
            weight[rows_of(u), :],
            (((1,), (1,)), ((), ())),
            preferred_element_type=jnp.float32,
        )
        part[u] = products.reshape(4, TOKENS, FEATURES)
        s_far[u] = part[u, shard(2)].astype(jnp.bfloat16)
        s_near[u] = part[u, shard(d)].astype(jnp.bfloat16)
        z_copy("far", u).start()
        z_copy("near", u).start()

    def pass_on(u):
        z_copy("far", u).wait_recv()
        s_mid[u] = (r_far[u].astype(jnp.float32) + part[u, shard(-way(u))]).astype(jnp.bfloat16)
        z_copy("mid", u).start()

    def own(u):
        z_copy("near", u).wait_recv()
        z_copy("mid", u).wait_recv()
        total = part[u, j] + r_near[u].astype(jnp.float32) + r_mid[u].astype(jnp.float32)
        cot[u, j] = (total - target[:, rows_of(u)].astype(jnp.float32)).astype(jnp.bfloat16)
        z_copy("ahead", u).start()
        z_copy("behind", u).start()

    def relay(u):
        z_copy("ahead", u).wait_recv()
        z_copy("relay", u).start()

    def gradients(u):
        z_copy("behind", u).wait_recv()
        z_copy("relay", u).wait_recv()
        whole = cot[u].reshape(4 * TOKENS, FEATURES)
        for first in range(0, WIDTH, 512):
            cols = slice(first, first + 512)
            rows = weight[rows_of(u), cols]
            grad = lax.dot_general(
                whole,
                normed[:, cols],
                (((0,), (0,)), ((), ())),
                preferred_element_type=jnp.float32,
            )
            moved = (rows.astype(jnp.float32) - inner_rate * grad).astype(jnp.bfloat16)
            fresh[u, :, :, :, cols] = moved.reshape(4, 2, 32, 512)
            d_normed[:, cols] += jnp.dot(whole, rows, preferred_element_type=jnp.float32)
        core_copy(u).start()

    def over_x(u):
        core_copy(u).wait_recv()
        for i in range(4):
            both = fresh[u, i, c].astype(jnp.float32) + r_core[u, i].astype(jnp.float32)
            s_core[u, i] = both.astype(jnp.bfloat16)
        for k in range(1, 4):
            x_copy(u, k).start()

    def after_x(u):
        total = s_core[u, x].astype(jnp.float32)
        for k in range(1, 4):
            x_copy(u, k).wait_recv()
            total = total + r_x[u, k - 1].astype(jnp.float32)
        s_x[u] = total.astype(jnp.bfloat16)

    d_normed[...] = jnp.zeros_like(d_normed)
    stages = list(zip((begin, pass_on, own, relay, gradients, over_x, after_x), LAGS))

    @pl.loop(0, UNITS + LAGS[-1])
    def _(k):
        for stage, lag in stages:

            @pl.when((k >= lag) & (k < UNITS + lag))
            def _():
                stage(k - lag)

    for half in range(2):
        for k in range(1, 4):
            y_copy(half, k).start()
    for half in range(2):
        total = s_x[half * 4 + y].astype(jnp.float32)
        for k in range(1, 4):
            y_copy(half, k).wait_recv()
            total = total + r_y[half, k - 1].astype(jnp.float32)
        s_y[half] = total
    s_z[...] = s_y[1 - zl].astype(jnp.bfloat16)
    over_z = remote(s_z, r_z, zl_send.at[0], zl_recv.at[0], on_z(1, 0))
    over_z.start()
    over_z.wait_recv()
    delta = global_own[...] - (s_y[zl] + r_z[...].astype(jnp.float32)) * (1.0 / 64)

    squares = jnp.sum((delta * delta).reshape(4, 8, WIDTH), axis=0)
    folded = squares[:, :128]
    for first in range(128, WIDTH, 128):
        folded = folded + squares[:, first : first + 128]
    sq_a[x, c] = folded
    a_copies = [
        remote(sq_a.at[x, c], sq_a.at[x, c], a_send.at[i], a_recv.at[i], on_x(*peer))
        for i, peer in enumerate(x_peers)
    ]
    for copy in a_copies:
        copy.start()
    for copy in a_copies:
        copy.wait_recv()
    sq_b[y] = jnp.sum(sq_a[...].reshape(8, 8, 128), axis=0)
    b_copies = [
        remote(sq_b.at[y], sq_b.at[y], b_send.at[k - 1], b_recv.at[k - 1], on_y(k))
        for k in range(1, 4)
    ]
    for copy in b_copies:
        copy.start()
    for copy in b_copies:
        copy.wait_recv()
    sq_c[zl, j] = jnp.sum(sq_b[...], axis=0)
    c_copies = [
        remote(sq_c.at[zl, j], sq_c.at[zl, j], c_send.at[i], c_recv.at[i], on_z(*peer))
        for i, peer in enumerate(z_peers)
    ]
    for copy in c_copies:
        copy.start()
    for copy in c_copies:
        copy.wait_recv()
    square_sum = jnp.sum(jnp.sum(sq_c[...].reshape(8, 8, 128), axis=0), keepdims=True)
    factor = jnp.minimum(1.0, clip_rms / jnp.sqrt(square_sum / ENTRIES + 1e-06))
    clipped = factor * delta
    moment = outer_beta * momentum_own[...] + clipped
    moved = global_own[...] - outer_rate * (clipped + outer_beta * moment)
    new_momentum[...] = moment
    new_global[...] = moved
    full[zl, y, x, c] = moved.astype(jnp.bfloat16)

    def gather(index, src, device):
        return remote(src, src, g_send.at[index], g_recv.at[index], device)

    mine = full.at[zl, y, x, c]
    first = gather(0, mine, on_z(1, 0))
    first.start()
    first.wait_recv()
    left, right = pl.ds(0, WIDTH // 2), pl.ds(WIDTH // 2, WIDTH // 2)
    near = [gather(k, full.at[:, y, x, c, :, left], on_y(k)) for k in range(1, 4)]
    near += [gather(3 + k, full.at[:, y, x, c, :, right], on_x(k, 0)) for k in range(1, 4)]
    for copy in near:
        copy.start()
    for copy in near:
        copy.wait_recv()
    far = [gather(6 + k, full.at[:, :, x, c, :, left], on_x(k, 0)) for k in range(1, 4)]
    far += [gather(9 + k, full.at[:, y, :, c, :, right], on_y(k)) for k in range(1, 4)]
    for i in (0, 3, 2, 5, 1, 4):
        far[i].start()

    def to_core(index, k):
        if index < 4:
            src = full.at[:, :, lax.rem(x + 4 - k, 4), c, :, left]
        else:
            src = full.at[:, lax.rem(y + 4 - k, 4), :, c, :, right]
        return gather(13 + index, src, on_x(0, 1))

    across = [to_core(0, 0), to_core(4, 0)]
    for copy in across:
        copy.start()
    for k in (1, 3, 2):
        for base in (0, 3):
            far[base + k - 1].wait_recv()
            copy = to_core(k if base == 0 else 4 + k, k)
            copy.start()
            across.append(copy)
    for copy in across:
        copy.wait_recv()

    for copy in [over_z, first, *a_copies, *b_copies, *c_copies, *near, *far, *across]:
        copy.wait_send()
    for half in range(2):
        for k in range(1, 4):
            y_copy(half, k).wait_send()

    @pl.loop(0, UNITS)
    def _(u):
        for kind in KINDS:
            z_copy(kind, u).wait_send()
        core_copy(u).wait_send()
        for k in range(1, 4):
            x_copy(u, k).wait_send()


def exchange(normed, weight, target, global_own, momentum_own):
    half = jnp.bfloat16
    piece = (UNITS, TOKENS, FEATURES)
    dma = pltpu.SemaphoreType.DMA
    vmem = pl.BlockSpec(memory_space=pltpu.VMEM)
    d_normed, full, new_global, new_momentum = pl.pallas_call(
        exchange_kernel,
        out_shape=(
            jax.ShapeDtypeStruct((4 * TOKENS, WIDTH), jnp.float32),
            jax.ShapeDtypeStruct((2, 4, 4, 2, 32, WIDTH), half),
            jax.ShapeDtypeStruct((32, WIDTH), jnp.float32),
            jax.ShapeDtypeStruct((32, WIDTH), jnp.float32),
        ),
        in_specs=[vmem] * 5,
        out_specs=[vmem] * 4,
        scratch_shapes=[
            pltpu.VMEM((UNITS, 4, TOKENS, FEATURES), jnp.float32),
            *[pltpu.VMEM(piece, half)] * 6,
            pltpu.VMEM((UNITS, 4, TOKENS, FEATURES), half),
            pltpu.VMEM((UNITS, 4, 2, 32, WIDTH), half),
            pltpu.VMEM((UNITS, 4, 32, WIDTH), half),
            pltpu.VMEM((UNITS, 4, 32, WIDTH), half),
            pltpu.VMEM((UNITS, 3, 32, WIDTH), half),
            pltpu.VMEM((UNITS, 32, WIDTH), half),
            pltpu.VMEM((2, 3, 32, WIDTH), half),
            pltpu.VMEM((2, 32, WIDTH), jnp.float32),
            pltpu.VMEM((32, WIDTH), half),
            pltpu.VMEM((32, WIDTH), half),
            pltpu.VMEM((4, 2, 8, 128), jnp.float32),
            pltpu.VMEM((4, 8, 128), jnp.float32),
            pltpu.VMEM((2, 4, 8, 128), jnp.float32),
            *[dma((UNITS, len(KINDS)))] * 2,
            *[dma((UNITS,))] * 2,
            *[dma((UNITS, 3))] * 2,
            *[dma((2, 3))] * 2,
            *[dma((1,))] * 2,
            *[dma((7,))] * 2,
            *[dma((3,))] * 2,
            *[dma((7,))] * 2,
            *[dma((21,))] * 2,
        ],
        compiler_params=pltpu.CompilerParams(
            collective_id=0, has_side_effects=True, vmem_limit_bytes=60 * 2**20
        ),
    )(normed, weight, target, global_own, momentum_own)
    return d_normed, full.reshape(2048, WIDTH), new_global, new_momentum


def head_scalars(ref, first, tokens):
    row = lax.broadcasted_iota(jnp.int32, (8, tokens), 0)
    out = jnp.zeros((8, tokens), jnp.float32)
    for r in range(8):
        out = jnp.where(row == r, ref[first + r], out)
    return out


def dot(a, b, over, **settings):
    return lax.dot_general(
        a, b, ((over[:1], over[1:]), ((), ())), preferred_element_type=jnp.float32, **settings
    )


def decays(dt, a_log, dt_bias, first):
    tokens = dt.shape[1]
    raw = dt[...] + head_scalars(dt_bias, first, tokens)
    step = jnp.maximum(raw, 0.0) + jnp.log1p(jnp.exp(-jnp.abs(raw)))
    rate = -jnp.exp(head_scalars(a_log, first, tokens)) * step
    below = lax.broadcasted_iota(jnp.int32, (SPAN, SPAN), 0) >= lax.broadcasted_iota(
        jnp.int32, (SPAN, SPAN), 1
    )
    ones = jnp.where(below, 1.0, 0.0)
    steps, by_row, by_column = [], [], []
    for k in range(2):
        own = rate[:, k * SPAN : (k + 1) * SPAN]
        steps.append(step[:, k * SPAN : (k + 1) * SPAN])
        by_row.append(dot(own, ones, (1, 1), precision=lax.Precision.HIGHEST))
        by_column.append(dot(ones, own, (1, 1), precision=lax.Precision.HIGHEST))
    return below, steps, by_row, by_column


def tail_keys(keys, step, cum):
    weight = jnp.exp(cum[:, SPAN - 1 :] - cum) * step
    turned = keys.astype(jnp.float32).T
    return [(turned * weight[r : r + 1]).astype(jnp.bfloat16) for r in range(8)]


def paired(low, one, two):
    return jnp.where(low, one, two)


def forward_kernel(
    a_log, dt_bias, skip, x_ref, z_ref, b_ref, c_ref, dt_ref, gain_ref, normed_ref, gated_ref, w_ref
):
    first = pl.program_id(0) * 8
    below, steps, by_row, by_column = decays(dt_ref, a_log, dt_bias, first)
    low = lax.broadcasted_iota(jnp.int32, (1, 128), 1) < HEAD_DIM
    tails = tail_keys(b_ref[:SPAN], steps[0], by_row[0])
    for k in range(2):
        rows = slice(k * SPAN, (k + 1) * SPAN)
        scores = dot(c_ref[rows], b_ref[rows], (1, 1))
        squares = jnp.zeros((SPAN, 1), jnp.float32)
        for q in range(4):
            cols = slice(q * 128, (q + 1) * 128)
            values = x_ref[rows, cols]
            sides = []
            for r in (2 * q, 2 * q + 1):
                gap = by_column[k][:, r : r + 1] - by_row[k][r : r + 1]
                table = jnp.where(below, jnp.exp(gap), 0.0)
                weights = (scores * table * steps[k][r : r + 1]).astype(jnp.bfloat16)
                w_ref[0, k, r] = weights
                sides.append(dot(weights, values, (1, 0)))
            skips = paired(low, skip[first + 2 * q], skip[first + 2 * q + 1])
            out = paired(low, *sides) + skips * values.astype(jnp.float32)
            if k == 1:
                earlier = x_ref[:SPAN, cols]
                state = paired(low, *[dot(tails[r], earlier, (1, 0)) for r in (2 * q, 2 * q + 1)])
                fade = jnp.exp(
                    paired(low, *[by_column[1][:, r : r + 1] for r in (2 * q, 2 * q + 1)])
                )
                out = out + dot(c_ref[rows], state.astype(jnp.bfloat16), (1, 0)) * fade
            z = z_ref[rows, cols].astype(jnp.float32)
            gated = out * (z / (1.0 + jnp.exp(-z)))
            gated_ref[rows, cols] = gated
            squares = squares + jnp.sum(gated * gated, axis=1, keepdims=True)
        scale = lax.rsqrt(squares * (1.0 / 512) + 1e-05)
        normed_ref[rows] = (gated_ref[rows] * scale * gain_ref[...]).astype(jnp.bfloat16)


def backward_kernel(
    a_log, dt_bias, skip, dn_ref, gated_ref, z_ref, w_ref, b_ref, c_ref, dt_ref, gain_ref, out_ref
):
    first = pl.program_id(0) * 8
    _, steps, by_row, by_column = decays(dt_ref, a_log, dt_bias, first)
    low = lax.broadcasted_iota(jnp.int32, (1, 128), 1) < HEAD_DIM
    tails = tail_keys(b_ref[:SPAN], steps[0], by_row[0])
    states = []
    for k in (1, 0):
        rows = slice(k * SPAN, (k + 1) * SPAN)
        gated = gated_ref[rows]
        pulled = dn_ref[rows] * gain_ref[...]
        mean = jnp.sum(gated * gated, axis=1, keepdims=True) * (1.0 / 512)
        scale = lax.rsqrt(mean + 1e-05)
        along = jnp.sum(gated * pulled, axis=1, keepdims=True) * (1.0 / 512)
        fall = along * scale * scale
        for q in range(4):
            cols = slice(q * 128, (q + 1) * 128)
            z = z_ref[rows, cols].astype(jnp.float32)
            own = dn_ref[rows, cols] * gain_ref[:, cols] - gated_ref[rows, cols] * fall
            ssd = own * scale * (z / (1.0 + jnp.exp(-z)))
            short = ssd.astype(jnp.bfloat16)
            sides = [dot(w_ref[0, k, r], short, (0, 0)) for r in (2 * q, 2 * q + 1)]
            skips = paired(low, skip[first + 2 * q], skip[first + 2 * q + 1])
            grad = paired(low, *sides) + skips * ssd
            if k == 1:
                fade = jnp.exp(
                    paired(low, *[by_column[1][:, r : r + 1] for r in (2 * q, 2 * q + 1)])
                )
                states.append(
                    dot(c_ref[rows], (ssd * fade).astype(jnp.bfloat16), (0, 0)).astype(
                        jnp.bfloat16
                    )
                )
            else:
                grad = grad + paired(
                    low, *[dot(tails[r], states[q], (0, 0)) for r in (2 * q, 2 * q + 1)]
                )
            out_ref[rows, cols] = grad.astype(jnp.bfloat16)


def group_specs():
    small = pl.BlockSpec(memory_space=pltpu.SMEM)
    wide = pl.BlockSpec((512, 512), lambda g: (0, g))
    state = pl.BlockSpec((512, STATE), lambda g: (0, g))
    heads = pl.BlockSpec((8, 512), lambda g: (g, 0))
    gain = pl.BlockSpec((1, 512), lambda g: (0, g))
    tables = pl.BlockSpec((1, 2, 8, SPAN, SPAN), lambda g: (g, 0, 0, 0, 0))
    return small, wide, state, heads, gain, tables


def forward(x_in, gate_z, b_proj, c_proj, dt, a_log, dt_bias, skip_d, gain_row):
    small, wide, state, heads, gain, tables = group_specs()
    return pl.pallas_call(
        forward_kernel,
        grid=(2,),
        out_shape=(
            jax.ShapeDtypeStruct((512, WIDTH), jnp.bfloat16),
            jax.ShapeDtypeStruct((512, WIDTH), jnp.float32),
            jax.ShapeDtypeStruct((2, 2, 8, SPAN, SPAN), jnp.bfloat16),
        ),
        in_specs=[small, small, small, wide, wide, state, state, heads, gain],
        out_specs=[wide, wide, tables],
        compiler_params=pltpu.CompilerParams(vmem_limit_bytes=48 * 2**20),
    )(a_log, dt_bias, skip_d, x_in, gate_z, b_proj, c_proj, dt, gain_row)


def pull_back(d_normed, gated, gate_z, tables_in, b_proj, c_proj, dt, a_log, dt_bias, skip_d, row):
    small, wide, state, heads, gain, tables = group_specs()
    return pl.pallas_call(
        backward_kernel,
        grid=(2,),
        out_shape=jax.ShapeDtypeStruct((512, WIDTH), jnp.bfloat16),
        in_specs=[small, small, small, wide, wide, wide, tables, state, state, heads, gain],
        out_specs=wide,
        compiler_params=pltpu.CompilerParams(vmem_limit_bytes=48 * 2**20),
    )(a_log, dt_bias, skip_d, d_normed, gated, gate_z, tables_in, b_proj, c_proj, dt, row)


def shards(
    x_in,
    gate_z,
    b_proj,
    c_proj,
    dt_raw,
    a_log,
    dt_bias,
    skip_d,
    norm_gain,
    out_weight,
    global_weight,
    momentum,
    target,
):
    local_weight = out_weight[0]

    dt = dt_raw.T
    gain_row = norm_gain.reshape(1, WIDTH)
    normed, gated, tables = forward(
        x_in, gate_z, b_proj, c_proj, dt, a_log, dt_bias, skip_d, gain_row
    )
    d_normed, new_weight, new_global, new_momentum = exchange(
        normed, local_weight, target, global_weight, momentum
    )
    grad_x = pull_back(
        d_normed, gated, gate_z, tables, b_proj, c_proj, dt, a_log, dt_bias, skip_d, gain_row
    )
    return (grad_x, new_weight, new_global, new_momentum)


def solution(mesh):
    torus = Mesh(
        mesh.devices.reshape(2, 4, 4, 2, mesh.shape["tensor"]),
        ("replica_0", "replica_1", "replica_2", "replica_3", "tensor"),
    )
    in_specs = (
        P(REPLICA, "tensor"),
        P(REPLICA, "tensor"),
        P(REPLICA, "tensor"),
        P(REPLICA, "tensor"),
        P(REPLICA, "tensor"),
        P("tensor"),
        P("tensor"),
        P("tensor"),
        P("tensor"),
        P(REPLICA, None, "tensor"),
        P(REPLICA, "tensor"),
        P(REPLICA, "tensor"),
        P(REPLICA_TENSOR, None),
    )
    out_specs = (
        P(REPLICA, "tensor"),
        P(None, "tensor"),
        P(REPLICA, "tensor"),
        P(REPLICA, "tensor"),
    )
    return jax.shard_map(
        shards, mesh=torus, in_specs=in_specs, out_specs=out_specs, check_vma=False
    )
```

```python
import jax
import jax.numpy as jnp
from jax import lax
from jax.experimental import pallas as pl
from jax.experimental.pallas import tpu as pltpu
from jax.sharding import Mesh
from jax.sharding import PartitionSpec as P

HEAD_DIM = 64
STATE = 128
SPAN = 256
REPLICA = ("replica_0", "replica_1", "replica_2", "replica_3")
REPLICA_TENSOR = ("replica_0", "replica_1", "replica_2", "replica_3", "tensor")


inner_rate = 0.001
outer_rate = 0.7
outer_beta = 0.9
clip_rms = 0.005
MESH = pl.DeviceIdType.MESH
UNITS = 8
FEATURES = 256
TOKENS = 128
WIDTH = 1024
ENTRIES = 2048 * 4096
KINDS = ("far", "near", "mid", "ahead", "behind", "relay")
LAGS = (0, 2, 3, 4, 5, 6, 7)


def exchange_kernel(
    normed,
    weight,
    target,
    global_own,
    momentum_own,
    d_normed,
    full,
    factor_out,
    new_global,
    new_momentum,
    part,
    s_far,
    s_near,
    s_mid,
    r_far,
    r_near,
    r_mid,
    cot,
    fresh,
    r_core,
    s_core,
    r_x,
    s_x,
    r_y,
    s_z,
    r_z,
    whole_global,
    delta,
    sq_a,
    sq_b,
    sq_c,
    z_send,
    z_recv,
    core_send,
    core_recv,
    x_send,
    x_recv,
    y_send,
    y_recv,
    zl_send,
    zl_recv,
    early_send,
    early_recv,
    a_send,
    a_recv,
    b_send,
    b_recv,
    c_send,
    c_recv,
    g_send,
    g_recv,
):
    zl = lax.axis_index("replica_0")
    y = lax.axis_index("replica_1")
    x = lax.axis_index("replica_2")
    c = lax.axis_index("replica_3")
    j = lax.axis_index("tensor")

    def on_z(kz, kj):
        return {"replica_0": lax.rem(zl + kz, 2), "tensor": lax.rem(j + kj, 4)}

    def on_x(kx, kc):
        return {"replica_2": lax.rem(x + kx, 4), "replica_3": lax.rem(c + kc, 2)}

    def on_y(ky):
        return {"replica_1": lax.rem(y + ky, 4)}

    z_peers = [(kz, kj) for kz in range(2) for kj in range(4) if kz + kj]
    x_peers = [(kx, kc) for kx in range(4) for kc in range(2) if kx + kc]
    barrier = pltpu.get_barrier_semaphore()
    for kz, kj in z_peers:
        pl.semaphore_signal(barrier, inc=1, device_id=on_z(kz, kj), device_id_type=MESH)
    for kx, kc in x_peers:
        pl.semaphore_signal(barrier, inc=1, device_id=on_x(kx, kc), device_id_type=MESH)
    for ky in range(1, 4):
        pl.semaphore_signal(barrier, inc=1, device_id=on_y(ky), device_id_type=MESH)
    pl.semaphore_wait(barrier, len(z_peers) + len(x_peers) + 3)

    def remote(src, dst, send_sem, recv_sem, device):
        return pltpu.make_async_remote_copy(
            src_ref=src,
            dst_ref=dst,
            send_sem=send_sem,
            recv_sem=recv_sem,
            device_id=device,
            device_id_type=MESH,
        )

    def way(u):
        return 1 - 2 * lax.rem(u, 2)

    def shard(step):
        return lax.rem(j + step + 4, 4)

    def z_copy(kind, u):
        d = way(u)
        ahead = {"tensor": shard(d)}
        behind = {"tensor": shard(-d)}
        src, dst, device = {
            "far": lambda: (s_far.at[u], r_far.at[u], behind),
            "near": lambda: (s_near.at[u], r_near.at[u], ahead),
            "mid": lambda: (s_mid.at[u], r_mid.at[u], behind),
            "ahead": lambda: (cot.at[u, j], cot.at[u, j], ahead),
            "behind": lambda: (cot.at[u, j], cot.at[u, j], behind),
            "relay": lambda: (cot.at[u, shard(-d)], cot.at[u, shard(-d)], ahead),
        }[kind]()
        slot = KINDS.index(kind)
        return remote(src, dst, z_send.at[u, slot], z_recv.at[u, slot], device)

    def core_copy(u):
        return remote(
            fresh.at[u, :, 1 - c],
            r_core.at[u],
            core_send.at[u],
            core_recv.at[u],
            {"replica_3": 1 - c},
        )

    def x_copy(u, k):
        there = lax.rem(x + k, 4)
        return remote(
            s_core.at[u, there],
            r_x.at[u, k - 1],
            x_send.at[u, k - 1],
            x_recv.at[u, k - 1],
            {"replica_2": there},
        )

    def y_copy(half, k):
        there = lax.rem(y + k, 4)
        return remote(
            s_x.at[half * 4 + there],
            r_y.at[half, k - 1],
            y_send.at[half, k - 1],
            y_recv.at[half, k - 1],
            {"replica_1": there},
        )

    def rows_of(u):
        return pl.ds(pl.multiple_of(u * FEATURES, FEATURES), FEATURES)

    def begin(u):
        d = way(u)
        products = lax.dot_general(
            normed[...],
            weight[rows_of(u), :],
            (((1,), (1,)), ((), ())),
            preferred_element_type=jnp.float32,
        )
        part[u] = products.reshape(4, TOKENS, FEATURES)
        s_far[u] = part[u, shard(2)].astype(jnp.bfloat16)
        s_near[u] = part[u, shard(d)].astype(jnp.bfloat16)
        z_copy("far", u).start()
        z_copy("near", u).start()

    def pass_on(u):
        z_copy("far", u).wait_recv()
        s_mid[u] = (r_far[u].astype(jnp.float32) + part[u, shard(-way(u))]).astype(jnp.bfloat16)
        z_copy("mid", u).start()

    def own(u):
        z_copy("near", u).wait_recv()
        z_copy("mid", u).wait_recv()
        total = part[u, j] + r_near[u].astype(jnp.float32) + r_mid[u].astype(jnp.float32)
        cot[u, j] = (total - target[:, rows_of(u)].astype(jnp.float32)).astype(jnp.bfloat16)
        z_copy("ahead", u).start()
        z_copy("behind", u).start()

    def relay(u):
        z_copy("ahead", u).wait_recv()
        z_copy("relay", u).start()

    def gradients(u):
        z_copy("behind", u).wait_recv()
        z_copy("relay", u).wait_recv()
        whole = cot[u].reshape(4 * TOKENS, FEATURES)
        for first in range(0, WIDTH, 512):
            cols = slice(first, first + 512)
            rows = weight[rows_of(u), cols]
            grad = lax.dot_general(
                whole,
                normed[:, cols],
                (((0,), (0,)), ((), ())),
                preferred_element_type=jnp.float32,
            )
            moved = (rows.astype(jnp.float32) - inner_rate * grad).astype(jnp.bfloat16)
            fresh[u, :, :, :, cols] = moved.reshape(4, 2, 32, 512)
            d_normed[:, cols] += jnp.dot(whole, rows, preferred_element_type=jnp.float32)
        core_copy(u).start()

    def over_x(u):
        core_copy(u).wait_recv()
        for i in range(4):
            both = fresh[u, i, c].astype(jnp.float32) + r_core[u, i].astype(jnp.float32)
            s_core[u, i] = both.astype(jnp.bfloat16)
        for k in range(1, 4):
            x_copy(u, k).start()

    def after_x(u):
        total = s_core[u, x].astype(jnp.float32)
        for k in range(1, 4):
            x_copy(u, k).wait_recv()
            total = total + r_x[u, k - 1].astype(jnp.float32)
        s_x[u] = total.astype(jnp.bfloat16)

    def zl_copy(half):
        return remote(s_z.at[half], r_z.at[half], zl_send.at[half], zl_recv.at[half], on_z(1, 0))

    def early_copies():
        base = full.at[0, zl, y, x, c]
        return (
            remote(base, base, early_send.at[0], early_recv.at[0], on_z(1, 0)),
            remote(
                global_own, whole_global.at[zl], early_send.at[1], early_recv.at[1], on_z(1, 0)
            ),
        )

    left, right = pl.ds(0, WIDTH // 2), pl.ds(WIDTH // 2, WIDTH // 2)

    def gather(which, half, index, src, device):
        row = which * 2 + half
        return remote(src, src, g_send.at[row, index], g_recv.at[row, index], device)

    def near_copies(which, half):
        piece = full.at[which, half]
        copies = []
        for k in range(1, 4):
            copies.append(gather(which, half, k - 1, piece.at[y, x, c, :, left], on_y(k)))
            copies.append(gather(which, half, k + 2, piece.at[y, x, c, :, right], on_x(k, 0)))
        return copies

    def far_copies(which, half, k):
        piece = full.at[which, half]
        return (
            gather(which, half, k + 5, piece.at[:, x, c, :, left], on_x(k, 0)),
            gather(which, half, k + 8, piece.at[y, :, c, :, right], on_y(k)),
        )

    def across_copies(which, half, k):
        piece = full.at[which, half]
        from_x, from_y = lax.rem(x + 4 - k, 4), lax.rem(y + 4 - k, 4)
        return (
            gather(which, half, 12 + k, piece.at[:, from_x, c, :, left], on_x(0, 1)),
            gather(which, half, 16 + k, piece.at[from_y, :, c, :, right], on_x(0, 1)),
        )

    def near_start(which, half):
        for copy in near_copies(which, half):
            copy.start()

    def far_start(which, half):
        for copy in near_copies(which, half):
            copy.wait_recv()
        for k in (1, 3, 2):
            for copy in far_copies(which, half, k):
                copy.start()
        for copy in across_copies(which, half, 0):
            copy.start()

    def across_start(which, half):
        for k in (1, 3, 2):
            for arrived, copy in zip(far_copies(which, half, k), across_copies(which, half, k)):
                arrived.wait_recv()
                copy.start()

    def y_start(half):
        for k in range(1, 4):
            y_copy(half, k).start()

    def after_y(half):
        total = s_x[half * 4 + y].astype(jnp.float32)
        for k in range(1, 4):
            y_copy(half, k).wait_recv()
            total = total + r_y[half, k - 1].astype(jnp.float32)
        s_z[half] = total.astype(jnp.bfloat16)
        zl_copy(half).start()

    def settle(half):
        zl_copy(half).wait_recv()
        total = s_z[half].astype(jnp.float32) + r_z[half].astype(jnp.float32)
        change = whole_global[half] - total * (1.0 / 64)
        delta[half] = change
        full[1, half, y, x, c] = change.astype(jnp.bfloat16)
        near_start(1, half)

    def early_near():
        for copy in early_copies():
            copy.wait_recv()
        near_start(0, 0)
        near_start(0, 1)

    def early_far():
        far_start(0, 0)
        far_start(0, 1)

    def early_across():
        across_start(0, 0)
        across_start(0, 1)

    whole_global[zl] = global_own[...]
    base = global_own[...] - (outer_rate * outer_beta * outer_beta) * momentum_own[...]
    full[0, zl, y, x, c] = base.astype(jnp.bfloat16)
    d_normed[...] = jnp.zeros_like(d_normed)
    for copy in early_copies():
        copy.start()
    stages = list(zip((begin, pass_on, own, relay, gradients, over_x, after_x), LAGS))
    middle = LAGS[-1] + UNITS // 2
    events = (
        (3, early_near),
        (4, early_far),
        (5, early_across),
        (middle, lambda: y_start(0)),
        (middle + 1, lambda: after_y(0)),
        (middle + 2, lambda: settle(0)),
        (middle + 3, lambda: far_start(1, 0)),
    )

    @pl.loop(0, UNITS + LAGS[-1])
    def _(k):
        for stage, lag in stages:

            @pl.when((k >= lag) & (k < UNITS + lag))
            def _():
                stage(k - lag)

        for when, event in events:

            @pl.when(k == when)
            def _():
                event()

    y_start(1)
    across_start(1, 0)
    after_y(1)
    settle(1)

    change = delta[zl]
    squares = jnp.sum((change * change).reshape(4, 8, WIDTH), axis=0)
    folded = squares[:, :128]
    for first in range(128, WIDTH, 128):
        folded = folded + squares[:, first : first + 128]
    sq_a[x, c] = folded
    a_copies = [
        remote(sq_a.at[x, c], sq_a.at[x, c], a_send.at[i], a_recv.at[i], on_x(*peer))
        for i, peer in enumerate(x_peers)
    ]
    for copy in a_copies:
        copy.start()
    for copy in a_copies:
        copy.wait_recv()
    sq_b[y] = jnp.sum(sq_a[...].reshape(8, 8, 128), axis=0)
    b_copies = [
        remote(sq_b.at[y], sq_b.at[y], b_send.at[k - 1], b_recv.at[k - 1], on_y(k))
        for k in range(1, 4)
    ]
    for copy in b_copies:
        copy.start()
    far_start(1, 1)
    for copy in b_copies:
        copy.wait_recv()
    sq_c[zl, j] = jnp.sum(sq_b[...], axis=0)
    c_copies = [
        remote(sq_c.at[zl, j], sq_c.at[zl, j], c_send.at[i], c_recv.at[i], on_z(*peer))
        for i, peer in enumerate(z_peers)
    ]
    for copy in c_copies:
        copy.start()
    across_start(1, 1)
    for copy in c_copies:
        copy.wait_recv()
    square_sum = jnp.sum(jnp.sum(sq_c[...].reshape(8, 8, 128), axis=0), keepdims=True)
    factor = jnp.minimum(1.0, clip_rms / jnp.sqrt(square_sum / ENTRIES + 1e-06))
    factor_out[...] = jnp.broadcast_to(factor, factor_out.shape)
    clipped = factor * change
    moment = outer_beta * momentum_own[...] + clipped
    new_momentum[...] = moment
    new_global[...] = global_own[...] - outer_rate * (clipped + outer_beta * moment)

    for copy in [*a_copies, *b_copies, *c_copies, *early_copies()]:
        copy.wait_send()
    for half in range(2):
        zl_copy(half).wait_send()
        for k in range(1, 4):
            y_copy(half, k).wait_send()
        for which in range(2):
            for copy in near_copies(which, half):
                copy.wait_send()
            for k in range(4):
                for copy in across_copies(which, half, k):
                    copy.wait()
                if k:
                    for copy in far_copies(which, half, k):
                        copy.wait_send()

    @pl.loop(0, UNITS)
    def _(u):
        for kind in KINDS:
            z_copy(kind, u).wait_send()
        core_copy(u).wait_send()
        for k in range(1, 4):
            x_copy(u, k).wait_send()


def exchange(normed, weight, target, global_own, momentum_own):
    half = jnp.bfloat16
    piece = (UNITS, TOKENS, FEATURES)
    dma = pltpu.SemaphoreType.DMA
    vmem = pl.BlockSpec(memory_space=pltpu.VMEM)
    d_normed, full, factor, new_global, new_momentum = pl.pallas_call(
        exchange_kernel,
        out_shape=(
            jax.ShapeDtypeStruct((4 * TOKENS, WIDTH), jnp.float32),
            jax.ShapeDtypeStruct((2, 2, 4, 4, 2, 32, WIDTH), half),
            jax.ShapeDtypeStruct((8, 128), jnp.float32),
            jax.ShapeDtypeStruct((32, WIDTH), jnp.float32),
            jax.ShapeDtypeStruct((32, WIDTH), jnp.float32),
        ),
        in_specs=[vmem] * 5,
        out_specs=[vmem] * 5,
        scratch_shapes=[
            pltpu.VMEM((UNITS, 4, TOKENS, FEATURES), jnp.float32),
            *[pltpu.VMEM(piece, half)] * 6,
            pltpu.VMEM((UNITS, 4, TOKENS, FEATURES), half),
            pltpu.VMEM((UNITS, 4, 2, 32, WIDTH), half),
            pltpu.VMEM((UNITS, 4, 32, WIDTH), half),
            pltpu.VMEM((UNITS, 4, 32, WIDTH), half),
            pltpu.VMEM((UNITS, 3, 32, WIDTH), half),
            pltpu.VMEM((UNITS, 32, WIDTH), half),
            pltpu.VMEM((2, 3, 32, WIDTH), half),
            pltpu.VMEM((2, 32, WIDTH), half),
            pltpu.VMEM((2, 32, WIDTH), half),
            pltpu.VMEM((2, 32, WIDTH), jnp.float32),
            pltpu.VMEM((2, 32, WIDTH), jnp.float32),
            pltpu.VMEM((4, 2, 8, 128), jnp.float32),
            pltpu.VMEM((4, 8, 128), jnp.float32),
            pltpu.VMEM((2, 4, 8, 128), jnp.float32),
            *[dma((UNITS, len(KINDS)))] * 2,
            *[dma((UNITS,))] * 2,
            *[dma((UNITS, 3))] * 2,
            *[dma((2, 3))] * 2,
            *[dma((2,))] * 2,
            *[dma((2,))] * 2,
            *[dma((7,))] * 2,
            *[dma((3,))] * 2,
            *[dma((7,))] * 2,
            *[dma((4, 20))] * 2,
        ],
        compiler_params=pltpu.CompilerParams(
            collective_id=0, has_side_effects=True, vmem_limit_bytes=67043328
        ),
    )(normed, weight, target, global_own, momentum_own)
    return d_normed, full.reshape(2, 2048, WIDTH), factor, new_global, new_momentum


def head_scalars(ref, first, tokens):
    row = lax.broadcasted_iota(jnp.int32, (8, tokens), 0)
    out = jnp.zeros((8, tokens), jnp.float32)
    for r in range(8):
        out = jnp.where(row == r, ref[first + r], out)
    return out


def dot(a, b, over, **settings):
    return lax.dot_general(
        a, b, ((over[:1], over[1:]), ((), ())), preferred_element_type=jnp.float32, **settings
    )


def decays(dt, a_log, dt_bias, first):
    tokens = dt.shape[1]
    raw = dt[...] + head_scalars(dt_bias, first, tokens)
    step = jnp.maximum(raw, 0.0) + jnp.log1p(jnp.exp(-jnp.abs(raw)))
    rate = -jnp.exp(head_scalars(a_log, first, tokens)) * step
    below = lax.broadcasted_iota(jnp.int32, (SPAN, SPAN), 0) >= lax.broadcasted_iota(
        jnp.int32, (SPAN, SPAN), 1
    )
    ones = jnp.where(below, 1.0, 0.0)
    steps, by_row, by_column = [], [], []
    for k in range(2):
        own = rate[:, k * SPAN : (k + 1) * SPAN]
        steps.append(step[:, k * SPAN : (k + 1) * SPAN])
        by_row.append(dot(own, ones, (1, 1), precision=lax.Precision.HIGHEST))
        by_column.append(dot(ones, own, (1, 1), precision=lax.Precision.HIGHEST))
    return below, steps, by_row, by_column


def tail_keys(keys, step, cum):
    weight = jnp.exp(cum[:, SPAN - 1 :] - cum) * step
    turned = keys.astype(jnp.float32).T
    return [(turned * weight[r : r + 1]).astype(jnp.bfloat16) for r in range(8)]


def paired(low, one, two):
    return jnp.where(low, one, two)


def forward_kernel(
    a_log, dt_bias, skip, x_ref, z_ref, b_ref, c_ref, dt_ref, gain_ref, normed_ref, gated_ref, w_ref
):
    first = pl.program_id(0) * 8
    below, steps, by_row, by_column = decays(dt_ref, a_log, dt_bias, first)
    low = lax.broadcasted_iota(jnp.int32, (1, 128), 1) < HEAD_DIM
    tails = tail_keys(b_ref[:SPAN], steps[0], by_row[0])
    for k in range(2):
        rows = slice(k * SPAN, (k + 1) * SPAN)
        scores = dot(c_ref[rows], b_ref[rows], (1, 1))
        squares = jnp.zeros((SPAN, 1), jnp.float32)
        for q in range(4):
            cols = slice(q * 128, (q + 1) * 128)
            values = x_ref[rows, cols]
            sides = []
            for r in (2 * q, 2 * q + 1):
                gap = by_column[k][:, r : r + 1] - by_row[k][r : r + 1]
                table = jnp.where(below, jnp.exp(gap), 0.0)
                weights = (scores * table * steps[k][r : r + 1]).astype(jnp.bfloat16)
                w_ref[0, k, r] = weights
                sides.append(dot(weights, values, (1, 0)))
            skips = paired(low, skip[first + 2 * q], skip[first + 2 * q + 1])
            out = paired(low, *sides) + skips * values.astype(jnp.float32)
            if k == 1:
                earlier = x_ref[:SPAN, cols]
                state = paired(low, *[dot(tails[r], earlier, (1, 0)) for r in (2 * q, 2 * q + 1)])
                fade = jnp.exp(
                    paired(low, *[by_column[1][:, r : r + 1] for r in (2 * q, 2 * q + 1)])
                )
                out = out + dot(c_ref[rows], state.astype(jnp.bfloat16), (1, 0)) * fade
            z = z_ref[rows, cols].astype(jnp.float32)
            gated = out * (z / (1.0 + jnp.exp(-z)))
            gated_ref[rows, cols] = gated
            squares = squares + jnp.sum(gated * gated, axis=1, keepdims=True)
        scale = lax.rsqrt(squares * (1.0 / 512) + 1e-05)
        normed_ref[rows] = (gated_ref[rows] * scale * gain_ref[...]).astype(jnp.bfloat16)


def backward_kernel(
    a_log,
    dt_bias,
    skip,
    dn_ref,
    gated_ref,
    z_ref,
    w_ref,
    b_ref,
    c_ref,
    dt_ref,
    gain_ref,
    pair_ref,
    factor_ref,
    global_ref,
    momentum_ref,
    out_ref,
    weight_ref,
    new_global,
    new_momentum,
):
    new_global[...] = global_ref[...]
    new_momentum[...] = momentum_ref[...]
    share = factor_ref[0:1, 0:1] * (outer_rate * (1.0 + outer_beta))

    @pl.loop(0, 16)
    def _(i):
        part = pl.ds(pl.multiple_of(i * 64, 64), 64)
        base = pair_ref[0, part].astype(jnp.float32)
        change = pair_ref[1, part].astype(jnp.float32)
        weight_ref[part] = (base - share * change).astype(jnp.bfloat16)

    first = pl.program_id(0) * 8
    _, steps, by_row, by_column = decays(dt_ref, a_log, dt_bias, first)
    low = lax.broadcasted_iota(jnp.int32, (1, 128), 1) < HEAD_DIM
    tails = tail_keys(b_ref[:SPAN], steps[0], by_row[0])
    states = []
    for k in (1, 0):
        rows = slice(k * SPAN, (k + 1) * SPAN)
        gated = gated_ref[rows]
        pulled = dn_ref[rows] * gain_ref[...]
        mean = jnp.sum(gated * gated, axis=1, keepdims=True) * (1.0 / 512)
        scale = lax.rsqrt(mean + 1e-05)
        along = jnp.sum(gated * pulled, axis=1, keepdims=True) * (1.0 / 512)
        fall = along * scale * scale
        for q in range(4):
            cols = slice(q * 128, (q + 1) * 128)
            z = z_ref[rows, cols].astype(jnp.float32)
            own = dn_ref[rows, cols] * gain_ref[:, cols] - gated_ref[rows, cols] * fall
            ssd = own * scale * (z / (1.0 + jnp.exp(-z)))
            short = ssd.astype(jnp.bfloat16)
            sides = [dot(w_ref[0, k, r], short, (0, 0)) for r in (2 * q, 2 * q + 1)]
            skips = paired(low, skip[first + 2 * q], skip[first + 2 * q + 1])
            grad = paired(low, *sides) + skips * ssd
            if k == 1:
                fade = jnp.exp(
                    paired(low, *[by_column[1][:, r : r + 1] for r in (2 * q, 2 * q + 1)])
                )
                states.append(
                    dot(c_ref[rows], (ssd * fade).astype(jnp.bfloat16), (0, 0)).astype(
                        jnp.bfloat16
                    )
                )
            else:
                grad = grad + paired(
                    low, *[dot(tails[r], states[q], (0, 0)) for r in (2 * q, 2 * q + 1)]
                )
            out_ref[rows, cols] = grad.astype(jnp.bfloat16)


def group_specs():
    small = pl.BlockSpec(memory_space=pltpu.SMEM)
    wide = pl.BlockSpec((512, 512), lambda g: (0, g))
    state = pl.BlockSpec((512, STATE), lambda g: (0, g))
    heads = pl.BlockSpec((8, 512), lambda g: (g, 0))
    gain = pl.BlockSpec((1, 512), lambda g: (0, g))
    tables = pl.BlockSpec((1, 2, 8, SPAN, SPAN), lambda g: (g, 0, 0, 0, 0))
    return small, wide, state, heads, gain, tables


def forward(x_in, gate_z, b_proj, c_proj, dt, a_log, dt_bias, skip_d, gain_row):
    small, wide, state, heads, gain, tables = group_specs()
    return pl.pallas_call(
        forward_kernel,
        grid=(2,),
        out_shape=(
            jax.ShapeDtypeStruct((512, WIDTH), jnp.bfloat16),
            jax.ShapeDtypeStruct((512, WIDTH), jnp.float32),
            jax.ShapeDtypeStruct((2, 2, 8, SPAN, SPAN), jnp.bfloat16),
        ),
        in_specs=[small, small, small, wide, wide, state, state, heads, gain],
        out_specs=[wide, wide, tables],
        compiler_params=pltpu.CompilerParams(vmem_limit_bytes=67043328),
    )(a_log, dt_bias, skip_d, x_in, gate_z, b_proj, c_proj, dt, gain_row)


def pull_back(
    d_normed, gated, gate_z, tables_in, b_proj, c_proj, dt, a_log, dt_bias, skip_d, row, *outer
):
    small, wide, state, heads, gain, tables = group_specs()
    rows = pl.BlockSpec((32, 512), lambda g: (0, g))
    return pl.pallas_call(
        backward_kernel,
        grid=(2,),
        out_shape=(
            jax.ShapeDtypeStruct((512, WIDTH), jnp.bfloat16),
            jax.ShapeDtypeStruct((2048, WIDTH), jnp.bfloat16),
            jax.ShapeDtypeStruct((32, WIDTH), jnp.float32),
            jax.ShapeDtypeStruct((32, WIDTH), jnp.float32),
        ),
        in_specs=[
            *[small, small, small, wide, wide, wide, tables, state, state, heads, gain],
            pl.BlockSpec((2, 1024, WIDTH), lambda g: (0, g, 0)),
            pl.BlockSpec((8, 128), lambda g: (0, 0)),
            rows,
            rows,
        ],
        out_specs=[wide, pl.BlockSpec((1024, WIDTH), lambda g: (g, 0)), rows, rows],
        compiler_params=pltpu.CompilerParams(vmem_limit_bytes=67043328),
    )(
        *[a_log, dt_bias, skip_d, d_normed, gated, gate_z, tables_in, b_proj, c_proj, dt, row],
        *outer,
    )


def shards(
    x_in,
    gate_z,
    b_proj,
    c_proj,
    dt_raw,
    a_log,
    dt_bias,
    skip_d,
    norm_gain,
    out_weight,
    global_weight,
    momentum,
    target,
):
    local_weight = out_weight[0]

    dt = dt_raw.T
    gain_row = norm_gain.reshape(1, WIDTH)
    normed, gated, tables = forward(
        x_in, gate_z, b_proj, c_proj, dt, a_log, dt_bias, skip_d, gain_row
    )
    d_normed, *outer = exchange(normed, local_weight, target, global_weight, momentum)
    grad_x, new_weight, new_global, new_momentum = pull_back(
        *[d_normed, gated, gate_z, tables, b_proj, c_proj, dt, a_log, dt_bias, skip_d],
        gain_row,
        *outer,
    )
    return (grad_x, new_weight, new_global, new_momentum)


def solution(mesh):
    torus = Mesh(
        mesh.devices.reshape(2, 4, 4, 2, mesh.shape["tensor"]),
        ("replica_0", "replica_1", "replica_2", "replica_3", "tensor"),
    )
    in_specs = (
        P(REPLICA, "tensor"),
        P(REPLICA, "tensor"),
        P(REPLICA, "tensor"),
        P(REPLICA, "tensor"),
        P(REPLICA, "tensor"),
        P("tensor"),
        P("tensor"),
        P("tensor"),
        P("tensor"),
        P(REPLICA, None, "tensor"),
        P(REPLICA, "tensor"),
        P(REPLICA, "tensor"),
        P(REPLICA_TENSOR, None),
    )
    out_specs = (
        P(REPLICA, "tensor"),
        P(None, "tensor"),
        P(REPLICA, "tensor"),
        P(REPLICA, "tensor"),
    )
    return jax.shard_map(
        shards, mesh=torus, in_specs=in_specs, out_specs=out_specs, check_vma=False
    )
```

```python
import jax
import jax.numpy as jnp
from jax import lax
from jax.experimental import pallas as pl
from jax.experimental.pallas import tpu as pltpu
from jax.sharding import Mesh
from jax.sharding import PartitionSpec as P

HEAD_DIM = 64
STATE = 128
SPAN = 256
REPLICA = ("replica_0", "replica_1", "replica_2", "replica_3")
REPLICA_TENSOR = ("replica_0", "replica_1", "replica_2", "replica_3", "tensor")


inner_rate = 0.001
outer_rate = 0.7
outer_beta = 0.9
clip_rms = 0.005
MESH = pl.DeviceIdType.MESH
UNITS = 8
FEATURES = 256
TOKENS = 128
WIDTH = 1024
ENTRIES = 2048 * 4096
KINDS = ("far", "near", "mid", "ahead", "behind", "relay")
ORDER = (
    ("begin", 0),
    ("begin", 1),
    ("begin", 2),
    ("begin", 3),
    ("begin", 4),
    ("pass", 0),
    ("begin", 5),
    ("begin", 6),
    ("pass", 2),
    ("early_near",),
    ("begin", 7),
    ("pass", 1),
    ("pass", 4),
    ("early_far",),
    ("own", 0),
    ("pass", 3),
    ("pass", 6),
    ("own", 2),
    ("pass", 5),
    ("early_across",),
    ("own", 4),
    ("pass", 7),
    ("own", 1),
    ("own", 6),
    ("relay", 0),
    ("own", 3),
    ("relay", 2),
    ("own", 5),
    ("relay", 1),
    ("relay", 4),
    ("own", 7),
    ("relay", 3),
    ("relay", 5),
    ("grad", 1),
    ("relay", 6),
    ("grad", 0),
    ("relay", 7),
    ("ox", 1),
    ("grad", 3),
    ("ox", 0),
    ("grad", 2),
    ("ox", 3),
    ("ax", 1),
    ("grad", 5),
    ("ox", 2),
    ("ax", 0),
    ("grad", 4),
    ("ox", 5),
    ("ax", 3),
    ("grad", 7),
    ("ox", 4),
    ("ax", 2),
    ("ys", 0),
    ("grad", 6),
    ("ox", 7),
    ("bwd", 1),
    ("ox", 6),
    ("ay", 0),
    ("ax", 4),
    ("ax", 5),
    ("bwd", 0),
    ("se", 0),
    ("ax", 7),
    ("ax", 6),
    ("ys", 1),
    ("far", 0),
    ("ay", 1),
    ("se", 1),
    ("a",),
    ("ac", 0),
    ("b",),
    ("far", 1),
    ("c",),
    ("fin",),
    ("ac", 1),
)


def head_scalars(ref, first, tokens):
    row = lax.broadcasted_iota(jnp.int32, (8, tokens), 0)
    out = jnp.zeros((8, tokens), jnp.float32)
    for r in range(8):
        out = jnp.where(row == r, ref[first + r], out)
    return out


def dot(a, b, over, **settings):
    return lax.dot_general(
        a, b, ((over[:1], over[1:]), ((), ())), preferred_element_type=jnp.float32, **settings
    )


def decays(dt, a_log, dt_bias, first):
    tokens = dt.shape[1]
    raw = dt[...] + head_scalars(dt_bias, first, tokens)
    step = jnp.maximum(raw, 0.0) + jnp.log1p(jnp.exp(-jnp.abs(raw)))
    rate = -jnp.exp(head_scalars(a_log, first, tokens)) * step
    below = lax.broadcasted_iota(jnp.int32, (SPAN, SPAN), 0) >= lax.broadcasted_iota(
        jnp.int32, (SPAN, SPAN), 1
    )
    ones = jnp.where(below, 1.0, 0.0)
    steps, by_row, by_column = [], [], []
    for k in range(2):
        own = rate[:, k * SPAN : (k + 1) * SPAN]
        steps.append(step[:, k * SPAN : (k + 1) * SPAN])
        by_row.append(dot(own, ones, (1, 1), precision=lax.Precision.HIGHEST))
        by_column.append(dot(ones, own, (1, 1), precision=lax.Precision.HIGHEST))
    return below, steps, by_row, by_column


def tail_keys(keys, step, cum):
    weight = jnp.exp(cum[:, SPAN - 1 :] - cum) * step
    turned = keys.astype(jnp.float32).T
    return [(turned * weight[r : r + 1]).astype(jnp.bfloat16) for r in range(8)]


def paired(low, one, two):
    return jnp.where(low, one, two)


def forward_group(
    g, a_log, dt_bias, skip, x_all, z_all, b_all, c_all, dt_all, gain_all, normed, gated_all, tables
):
    first = g * 8
    wide = pl.ds(pl.multiple_of(g * 512, 512), 512)
    narrow = pl.ds(pl.multiple_of(g * STATE, STATE), STATE)
    x_ref, z_ref = x_all.at[:, wide], z_all.at[:, wide]
    b_ref, c_ref = b_all.at[:, narrow], c_all.at[:, narrow]
    dt_ref = dt_all.at[pl.ds(pl.multiple_of(first, 8), 8)]
    gain_ref, normed_ref, gated_ref = gain_all.at[:, wide], normed.at[:, wide], gated_all.at[:, wide]
    below, steps, by_row, by_column = decays(dt_ref, a_log, dt_bias, first)
    low = lax.broadcasted_iota(jnp.int32, (1, 128), 1) < HEAD_DIM
    tails = tail_keys(b_ref[:SPAN], steps[0], by_row[0])
    for k in range(2):
        rows = slice(k * SPAN, (k + 1) * SPAN)
        scores = dot(c_ref[rows], b_ref[rows], (1, 1))
        squares = jnp.zeros((SPAN, 1), jnp.float32)
        for q in range(4):
            cols = slice(q * 128, (q + 1) * 128)
            values = x_ref[rows, cols]
            sides = []
            for r in (2 * q, 2 * q + 1):
                gap = by_column[k][:, r : r + 1] - by_row[k][r : r + 1]
                table = jnp.where(below, jnp.exp(gap), 0.0)
                weights = (scores * table * steps[k][r : r + 1]).astype(jnp.bfloat16)
                tables[g, k, r] = weights
                sides.append(dot(weights, values, (1, 0)))
            skips = paired(low, skip[first + 2 * q], skip[first + 2 * q + 1])
            out = paired(low, *sides) + skips * values.astype(jnp.float32)
            if k == 1:
                earlier = x_ref[:SPAN, cols]
                state = paired(low, *[dot(tails[r], earlier, (1, 0)) for r in (2 * q, 2 * q + 1)])
                fade = jnp.exp(
                    paired(low, *[by_column[1][:, r : r + 1] for r in (2 * q, 2 * q + 1)])
                )
                out = out + dot(c_ref[rows], state.astype(jnp.bfloat16), (1, 0)) * fade
            z = z_ref[rows, cols].astype(jnp.float32)
            gated = out * (z / (1.0 + jnp.exp(-z)))
            gated_ref[rows, cols] = gated
            squares = squares + jnp.sum(gated * gated, axis=1, keepdims=True)
        scale = lax.rsqrt(squares * (1.0 / 512) + 1e-05)
        normed_ref[rows] = (gated_ref[rows] * scale * gain_ref[...]).astype(jnp.bfloat16)


def backward_group(
    g, a_log, dt_bias, skip, dn_all, gated_all, z_all, tables, b_all, c_all, dt_all, gain_all, grad
):
    first = g * 8
    wide, narrow = slice(g * 512, g * 512 + 512), slice(g * STATE, g * STATE + STATE)
    dn_ref, gated_ref, z_ref = dn_all.at[:, wide], gated_all.at[:, wide], z_all.at[:, wide]
    b_ref, c_ref, dt_ref = b_all.at[:, narrow], c_all.at[:, narrow], dt_all.at[first : first + 8]
    gain_ref, out_ref = gain_all.at[:, wide], grad.at[:, wide]
    _, steps, by_row, by_column = decays(dt_ref, a_log, dt_bias, first)
    low = lax.broadcasted_iota(jnp.int32, (1, 128), 1) < HEAD_DIM
    tails = tail_keys(b_ref[:SPAN], steps[0], by_row[0])
    states = []
    for k in (1, 0):
        rows = slice(k * SPAN, (k + 1) * SPAN)
        gated = gated_ref[rows]
        pulled = dn_ref[rows] * gain_ref[...]
        mean = jnp.sum(gated * gated, axis=1, keepdims=True) * (1.0 / 512)
        scale = lax.rsqrt(mean + 1e-05)
        along = jnp.sum(gated * pulled, axis=1, keepdims=True) * (1.0 / 512)
        fall = along * scale * scale
        for q in range(4):
            cols = slice(q * 128, (q + 1) * 128)
            z = z_ref[rows, cols].astype(jnp.float32)
            own = dn_ref[rows, cols] * gain_ref[:, cols] - gated_ref[rows, cols] * fall
            ssd = own * scale * (z / (1.0 + jnp.exp(-z)))
            short = ssd.astype(jnp.bfloat16)
            sides = [dot(tables[g, k, r], short, (0, 0)) for r in (2 * q, 2 * q + 1)]
            skips = paired(low, skip[first + 2 * q], skip[first + 2 * q + 1])
            grad = paired(low, *sides) + skips * ssd
            if k == 1:
                fade = jnp.exp(
                    paired(low, *[by_column[1][:, r : r + 1] for r in (2 * q, 2 * q + 1)])
                )
                states.append(
                    dot(c_ref[rows], (ssd * fade).astype(jnp.bfloat16), (0, 0)).astype(
                        jnp.bfloat16
                    )
                )
            else:
                grad = grad + paired(
                    low, *[dot(tails[r], states[q], (0, 0)) for r in (2 * q, 2 * q + 1)]
                )
            out_ref[rows, cols] = grad.astype(jnp.bfloat16)


def step_kernel(
    a_log,
    dt_bias,
    skip,
    x_ref,
    z_ref,
    b_ref,
    c_ref,
    dt_ref,
    gain_ref,
    weight_in,
    target,
    global_own,
    momentum_own,
    grad_x,
    new_weight,
    new_global,
    new_momentum,
    weight,
    normed,
    gated,
    tables,
    d_normed,
    full,
    part,
    s_far,
    s_near,
    s_mid,
    r_far,
    r_near,
    r_mid,
    cot,
    fresh,
    r_core,
    s_core,
    r_x,
    s_x,
    r_y,
    s_z,
    r_z,
    whole_global,
    delta,
    sq_a,
    sq_b,
    sq_c,
    share,
    weight_sem,
    z_send,
    z_recv,
    core_send,
    core_recv,
    x_send,
    x_recv,
    y_send,
    y_recv,
    zl_send,
    zl_recv,
    early_send,
    early_recv,
    a_send,
    a_recv,
    b_send,
    b_recv,
    c_send,
    c_recv,
    g_send,
    g_recv,
):
    zl = lax.axis_index("replica_0")
    y = lax.axis_index("replica_1")
    x = lax.axis_index("replica_2")
    c = lax.axis_index("replica_3")
    j = lax.axis_index("tensor")

    def on_z(kz, kj):
        return {"replica_0": lax.rem(zl + kz, 2), "tensor": lax.rem(j + kj, 4)}

    def on_x(kx, kc):
        return {"replica_2": lax.rem(x + kx, 4), "replica_3": lax.rem(c + kc, 2)}

    def on_y(ky):
        return {"replica_1": lax.rem(y + ky, 4)}

    z_peers = [(kz, kj) for kz in range(2) for kj in range(4) if kz + kj]
    x_peers = [(kx, kc) for kx in range(4) for kc in range(2) if kx + kc]
    barrier = pltpu.get_barrier_semaphore()
    for kz, kj in z_peers:
        pl.semaphore_signal(barrier, inc=1, device_id=on_z(kz, kj), device_id_type=MESH)
    for kx, kc in x_peers:
        pl.semaphore_signal(barrier, inc=1, device_id=on_x(kx, kc), device_id_type=MESH)
    for ky in range(1, 4):
        pl.semaphore_signal(barrier, inc=1, device_id=on_y(ky), device_id_type=MESH)
    fetch = pltpu.make_async_copy(weight_in, weight, weight_sem)
    fetch.start()

    @pl.loop(0, 2)
    def _(g):
        forward_group(
            *[g, a_log, dt_bias, skip, x_ref, z_ref, b_ref, c_ref, dt_ref, gain_ref],
            *[normed, gated, tables],
        )

    pl.semaphore_wait(barrier, len(z_peers) + len(x_peers) + 3)
    fetch.wait()

    def remote(src, dst, send_sem, recv_sem, device):
        return pltpu.make_async_remote_copy(
            src_ref=src,
            dst_ref=dst,
            send_sem=send_sem,
            recv_sem=recv_sem,
            device_id=device,
            device_id_type=MESH,
        )

    def way(u):
        return 1 - 2 * (u % 2)

    def shard(step):
        return lax.rem(j + step + 4, 4)

    def z_copy(kind, u):
        d = way(u)
        ahead = {"tensor": shard(d)}
        behind = {"tensor": shard(-d)}
        src, dst, device = {
            "far": lambda: (s_far.at[u], r_far.at[u], behind),
            "near": lambda: (s_near.at[u], r_near.at[u], ahead),
            "mid": lambda: (s_mid.at[u], r_mid.at[u], behind),
            "ahead": lambda: (cot.at[u, j], cot.at[u, j], ahead),
            "behind": lambda: (cot.at[u, j], cot.at[u, j], behind),
            "relay": lambda: (cot.at[u, shard(-d)], cot.at[u, shard(-d)], ahead),
        }[kind]()
        slot = KINDS.index(kind)
        return remote(src, dst, z_send.at[u, slot], z_recv.at[u, slot], device)

    def core_copy(u):
        return remote(
            fresh.at[u, :, 1 - c],
            r_core.at[u],
            core_send.at[u],
            core_recv.at[u],
            {"replica_3": 1 - c},
        )

    def x_copy(u, k):
        there = lax.rem(x + k, 4)
        return remote(
            s_core.at[u, there],
            r_x.at[u, k - 1],
            x_send.at[u, k - 1],
            x_recv.at[u, k - 1],
            {"replica_2": there},
        )

    def y_copy(half, k):
        there = lax.rem(y + k, 4)
        return remote(
            s_x.at[half * 4 + there],
            r_y.at[half, k - 1],
            y_send.at[half, k - 1],
            y_recv.at[half, k - 1],
            {"replica_1": there},
        )

    def rows_of(u):
        return slice(u * FEATURES, (u + 1) * FEATURES)

    def begin(u):
        d = way(u)
        products = lax.dot_general(
            normed[...],
            weight[rows_of(u), :],
            (((1,), (1,)), ((), ())),
            preferred_element_type=jnp.float32,
        )
        part[u] = products.reshape(4, TOKENS, FEATURES)
        s_far[u] = part[u, shard(2)].astype(jnp.bfloat16)
        s_near[u] = part[u, shard(d)].astype(jnp.bfloat16)
        z_copy("far", u).start()
        z_copy("near", u).start()

    def pass_on(u):
        z_copy("far", u).wait_recv()
        s_mid[u] = (r_far[u].astype(jnp.float32) + part[u, shard(-way(u))]).astype(jnp.bfloat16)
        z_copy("mid", u).start()

    def own(u):
        z_copy("near", u).wait_recv()
        z_copy("mid", u).wait_recv()
        total = part[u, j] + r_near[u].astype(jnp.float32) + r_mid[u].astype(jnp.float32)
        cot[u, j] = (total - target[:, rows_of(u)].astype(jnp.float32)).astype(jnp.bfloat16)
        z_copy("ahead", u).start()
        z_copy("behind", u).start()

    def relay(u):
        z_copy("ahead", u).wait_recv()
        z_copy("relay", u).start()

    def gradients(u):
        z_copy("behind", u).wait_recv()
        z_copy("relay", u).wait_recv()
        whole = cot[u].reshape(4 * TOKENS, FEATURES)
        for first in range(0, WIDTH, 512):
            cols = slice(first, first + 512)
            rows = weight[rows_of(u), cols]
            grad = lax.dot_general(
                whole,
                normed[:, cols],
                (((0,), (0,)), ((), ())),
                preferred_element_type=jnp.float32,
            )
            moved = (rows.astype(jnp.float32) - inner_rate * grad).astype(jnp.bfloat16)
            fresh[u, :, :, :, cols] = moved.reshape(4, 2, 32, 512)
            d_normed[:, cols] += jnp.dot(whole, rows, preferred_element_type=jnp.float32)
        core_copy(u).start()

    def over_x(u):
        core_copy(u).wait_recv()
        for i in range(4):
            both = fresh[u, i, c].astype(jnp.float32) + r_core[u, i].astype(jnp.float32)
            s_core[u, i] = both.astype(jnp.bfloat16)
        for k in range(1, 4):
            x_copy(u, k).start()

    def after_x(u):
        total = s_core[u, x].astype(jnp.float32)
        for k in range(1, 4):
            x_copy(u, k).wait_recv()
            total = total + r_x[u, k - 1].astype(jnp.float32)
        s_x[u] = total.astype(jnp.bfloat16)

    def zl_copy(half):
        return remote(s_z.at[half], r_z.at[half], zl_send.at[half], zl_recv.at[half], on_z(1, 0))

    def early_copies():
        base = full.at[0, zl, y, x, c]
        return (
            remote(base, base, early_send.at[0], early_recv.at[0], on_z(1, 0)),
            remote(
                global_own, whole_global.at[zl], early_send.at[1], early_recv.at[1], on_z(1, 0)
            ),
        )

    left, right = pl.ds(0, WIDTH // 2), pl.ds(WIDTH // 2, WIDTH // 2)

    def gather(which, half, index, src, device):
        row = which * 2 + half
        return remote(src, src, g_send.at[row, index], g_recv.at[row, index], device)

    def near_copies(which, half):
        piece = full.at[which, half]
        copies = []
        for k in range(1, 4):
            copies.append(gather(which, half, k - 1, piece.at[y, x, c, :, left], on_y(k)))
            copies.append(gather(which, half, k + 2, piece.at[y, x, c, :, right], on_x(k, 0)))
        return copies

    def far_copies(which, half, k):
        piece = full.at[which, half]
        return (
            gather(which, half, k + 5, piece.at[:, x, c, :, left], on_x(k, 0)),
            gather(which, half, k + 8, piece.at[y, :, c, :, right], on_y(k)),
        )

    def across_copies(which, half, k):
        piece = full.at[which, half]
        from_x, from_y = lax.rem(x + 4 - k, 4), lax.rem(y + 4 - k, 4)
        return (
            gather(which, half, 12 + k, piece.at[:, from_x, c, :, left], on_x(0, 1)),
            gather(which, half, 16 + k, piece.at[from_y, :, c, :, right], on_x(0, 1)),
        )

    def near_start(which, half):
        for copy in near_copies(which, half):
            copy.start()

    def far_start(which, half):
        for copy in near_copies(which, half):
            copy.wait_recv()
        for k in (1, 3, 2):
            for copy in far_copies(which, half, k):
                copy.start()
        for copy in across_copies(which, half, 0):
            copy.start()

    def across_start(which, half):
        for k in (1, 3, 2):
            for arrived, copy in zip(far_copies(which, half, k), across_copies(which, half, k)):
                arrived.wait_recv()
                copy.start()

    def y_start(half):
        for k in range(1, 4):
            y_copy(half, k).start()

    def after_y(half):
        total = s_x[half * 4 + y].astype(jnp.float32)
        for k in range(1, 4):
            y_copy(half, k).wait_recv()
            total = total + r_y[half, k - 1].astype(jnp.float32)
        s_z[half] = total.astype(jnp.bfloat16)
        zl_copy(half).start()

    def settle(half):
        zl_copy(half).wait_recv()
        total = s_z[half].astype(jnp.float32) + r_z[half].astype(jnp.float32)
        change = whole_global[half] - total * (1.0 / 64)
        delta[half] = change
        full[1, half, y, x, c] = change.astype(jnp.bfloat16)
        near_start(1, half)

    def early_near():
        for copy in early_copies():
            copy.wait_recv()
        near_start(0, 0)
        near_start(0, 1)

    def early_far():
        far_start(0, 0)
        far_start(0, 1)

    def early_across():
        across_start(0, 0)
        across_start(0, 1)

    whole_global[zl] = global_own[...]
    base = global_own[...] - (outer_rate * outer_beta * outer_beta) * momentum_own[...]
    full[0, zl, y, x, c] = base.astype(jnp.bfloat16)
    d_normed[...] = jnp.zeros_like(d_normed)
    for copy in early_copies():
        copy.start()
    def sum_a():
        change = delta[zl]
        squares = jnp.sum((change * change).reshape(4, 8, WIDTH), axis=0)
        folded = squares[:, :128]
        for first in range(128, WIDTH, 128):
            folded = folded + squares[:, first : first + 128]
        sq_a[x, c] = folded
        for copy in a_copies:
            copy.start()

    def sum_b():
        for copy in a_copies:
            copy.wait_recv()
        sq_b[y] = jnp.sum(sq_a[...].reshape(8, 8, 128), axis=0)
        for copy in b_copies:
            copy.start()

    def sum_c():
        for copy in b_copies:
            copy.wait_recv()
        sq_c[zl, j] = jnp.sum(sq_b[...], axis=0)
        for copy in c_copies:
            copy.start()

    def apply(half, share):
        for k in range(4):
            for which in range(2):
                for copy in across_copies(which, half, k):
                    copy.wait_recv()

        @pl.loop(0, 16)
        def _(i):
            row, column = lax.div(i, 4), lax.rem(i, 4)
            base = full[0, half, row, column].astype(jnp.float32)
            moved = base - share * full[1, half, row, column].astype(jnp.float32)
            new_weight[half, row, column] = moved.astype(jnp.bfloat16)

    def finish():
        for copy in c_copies:
            copy.wait_recv()
        square_sum = jnp.sum(jnp.sum(sq_c[...].reshape(8, 8, 128), axis=0), keepdims=True)
        factor = jnp.minimum(1.0, clip_rms / jnp.sqrt(square_sum / ENTRIES + 1e-06))
        clipped = factor * delta[zl]
        moment = outer_beta * momentum_own[...] + clipped
        new_momentum[...] = moment
        new_global[...] = global_own[...] - outer_rate * (clipped + outer_beta * moment)
        share[...] = jnp.broadcast_to(factor * (outer_rate * (1.0 + outer_beta)), share.shape)

    def backward(g):
        backward_group(
            *[g, a_log, dt_bias, skip, d_normed, gated, z_ref, tables],
            *[b_ref, c_ref, dt_ref, gain_ref, grad_x],
        )

    a_copies = [
        remote(sq_a.at[x, c], sq_a.at[x, c], a_send.at[i], a_recv.at[i], on_x(*peer))
        for i, peer in enumerate(x_peers)
    ]
    b_copies = [
        remote(sq_b.at[y], sq_b.at[y], b_send.at[k - 1], b_recv.at[k - 1], on_y(k))
        for k in range(1, 4)
    ]
    c_copies = [
        remote(sq_c.at[zl, j], sq_c.at[zl, j], c_send.at[i], c_recv.at[i], on_z(*peer))
        for i, peer in enumerate(z_peers)
    ]
    actions = {
        "begin": begin,
        "pass": pass_on,
        "own": own,
        "relay": relay,
        "grad": gradients,
        "ox": over_x,
        "ax": after_x,
        "early_near": early_near,
        "early_far": early_far,
        "early_across": early_across,
        "ys": y_start,
        "ay": after_y,
        "se": settle,
        "far": lambda half: far_start(1, half),
        "ac": lambda half: across_start(1, half),
        "a": sum_a,
        "b": sum_b,
        "c": sum_c,
        "fin": finish,
        "bwd": backward,
    }
    for name, *index in ORDER:
        actions[name](*index)
    for half in range(2):
        apply(half, share[0:1, 0:1])

    for copy in [*a_copies, *b_copies, *c_copies, *early_copies()]:
        copy.wait_send()
    for half in range(2):
        zl_copy(half).wait_send()
        for k in range(1, 4):
            y_copy(half, k).wait_send()
        for which in range(2):
            for copy in near_copies(which, half):
                copy.wait_send()
            for k in range(4):
                for copy in across_copies(which, half, k):
                    copy.wait_send()
                if k:
                    for copy in far_copies(which, half, k):
                        copy.wait_send()

    for u in range(UNITS):
        for kind in KINDS:
            z_copy(kind, u).wait_send()
        core_copy(u).wait_send()
        for k in range(1, 4):
            x_copy(u, k).wait_send()


def step(a_log, dt_bias, skip, x_in, gate_z, b_proj, c_proj, dt, gain, weight, target, *outer):
    half = jnp.bfloat16
    piece = (UNITS, TOKENS, FEATURES)
    dma = pltpu.SemaphoreType.DMA
    vmem = pl.BlockSpec(memory_space=pltpu.VMEM)
    smem = pl.BlockSpec(memory_space=pltpu.SMEM)
    grad_x, new_weight, new_global, new_momentum = pl.pallas_call(
        step_kernel,
        out_shape=(
            jax.ShapeDtypeStruct((512, WIDTH), half),
            jax.ShapeDtypeStruct((2, 4, 4, 2, 32, WIDTH), half),
            jax.ShapeDtypeStruct((32, WIDTH), jnp.float32),
            jax.ShapeDtypeStruct((32, WIDTH), jnp.float32),
        ),
        in_specs=[*[smem] * 3, *[vmem] * 6, pl.BlockSpec(memory_space=pl.ANY), *[vmem] * 3],
        out_specs=[vmem] * 4,
        scratch_shapes=[
            pltpu.VMEM((2048, WIDTH), half),
            pltpu.VMEM((512, WIDTH), half),
            pltpu.VMEM((512, WIDTH), jnp.float32),
            pltpu.VMEM((2, 2, 8, SPAN, SPAN), half),
            pltpu.VMEM((512, WIDTH), jnp.float32),
            pltpu.VMEM((2, 2, 4, 4, 2, 32, WIDTH), half),
            pltpu.VMEM((UNITS, 4, TOKENS, FEATURES), jnp.float32),
            *[pltpu.VMEM(piece, half)] * 6,
            pltpu.VMEM((UNITS, 4, TOKENS, FEATURES), half),
            pltpu.VMEM((UNITS, 4, 2, 32, WIDTH), half),
            pltpu.VMEM((UNITS, 4, 32, WIDTH), half),
            pltpu.VMEM((UNITS, 4, 32, WIDTH), half),
            pltpu.VMEM((UNITS, 3, 32, WIDTH), half),
            pltpu.VMEM((UNITS, 32, WIDTH), half),
            pltpu.VMEM((2, 3, 32, WIDTH), half),
            pltpu.VMEM((2, 32, WIDTH), half),
            pltpu.VMEM((2, 32, WIDTH), half),
            pltpu.VMEM((2, 32, WIDTH), jnp.float32),
            pltpu.VMEM((2, 32, WIDTH), jnp.float32),
            pltpu.VMEM((4, 2, 8, 128), jnp.float32),
            pltpu.VMEM((4, 8, 128), jnp.float32),
            pltpu.VMEM((2, 4, 8, 128), jnp.float32),
            pltpu.VMEM((8, 128), jnp.float32),
            dma,
            *[dma((UNITS, len(KINDS)))] * 2,
            *[dma((UNITS,))] * 2,
            *[dma((UNITS, 3))] * 2,
            *[dma((2, 3))] * 2,
            *[dma((2,))] * 2,
            *[dma((2,))] * 2,
            *[dma((7,))] * 2,
            *[dma((3,))] * 2,
            *[dma((7,))] * 2,
            *[dma((4, 20))] * 2,
        ],
        compiler_params=pltpu.CompilerParams(
            collective_id=0, has_side_effects=True, vmem_limit_bytes=67043328
        ),
    )(a_log, dt_bias, skip, x_in, gate_z, b_proj, c_proj, dt, gain, weight, target, *outer)
    return grad_x, new_weight.reshape(2048, WIDTH), new_global, new_momentum


def shards(
    x_in,
    gate_z,
    b_proj,
    c_proj,
    dt_raw,
    a_log,
    dt_bias,
    skip_d,
    norm_gain,
    out_weight,
    global_weight,
    momentum,
    target,
):
    return step(
        *[a_log, dt_bias, skip_d, x_in, gate_z, b_proj, c_proj, dt_raw.T],
        *[norm_gain.reshape(1, WIDTH), out_weight[0], target, global_weight, momentum],
    )


def solution(mesh):
    torus = Mesh(
        mesh.devices.reshape(2, 4, 4, 2, mesh.shape["tensor"]),
        ("replica_0", "replica_1", "replica_2", "replica_3", "tensor"),
    )
    in_specs = (
        P(REPLICA, "tensor"),
        P(REPLICA, "tensor"),
        P(REPLICA, "tensor"),
        P(REPLICA, "tensor"),
        P(REPLICA, "tensor"),
        P("tensor"),
        P("tensor"),
        P("tensor"),
        P("tensor"),
        P(REPLICA, None, "tensor"),
        P(REPLICA, "tensor"),
        P(REPLICA, "tensor"),
        P(REPLICA_TENSOR, None),
    )
    out_specs = (
        P(REPLICA, "tensor"),
        P(None, "tensor"),
        P(REPLICA, "tensor"),
        P(REPLICA, "tensor"),
    )
    return jax.shard_map(
        shards, mesh=torus, in_specs=in_specs, out_specs=out_specs, check_vma=False
    )
```

```python
import jax
import jax.numpy as jnp
from jax import lax
from jax.experimental import pallas as pl
from jax.experimental.pallas import tpu as pltpu
from jax.sharding import Mesh
from jax.sharding import PartitionSpec as P

HEAD_DIM = 64
STATE = 128
SPAN = 256
REPLICA = ("replica_0", "replica_1", "replica_2", "replica_3")
REPLICA_TENSOR = ("replica_0", "replica_1", "replica_2", "replica_3", "tensor")


inner_rate = 0.001
outer_rate = 0.7
outer_beta = 0.9
clip_rms = 0.005
MESH = pl.DeviceIdType.MESH
UNITS = 8
FEATURES = 256
TOKENS = 128
WIDTH = 1024
ENTRIES = 2048 * 4096
KINDS = ("far", "near", "mid", "ahead", "behind", "relay")
ORDER = (
    ("begin", 0),
    ("begin", 1),
    ("begin", 2),
    ("pass", 0),
    ("early_near",),
    ("pass", 1),
    ("begin", 3),
    ("pass", 2),
    ("begin", 4),
    ("own", 0),
    ("own", 1),
    ("pass", 3),
    ("early_far",),
    ("own", 2),
    ("relay", 0),
    ("pass", 4),
    ("relay", 1),
    ("own", 3),
    ("relay", 2),
    ("grad", 0),
    ("begin", 5),
    ("begin", 6),
    ("ox", 0),
    ("grad", 1),
    ("begin", 7),
    ("relay", 3),
    ("ox", 1),
    ("grad", 2),
    ("own", 4),
    ("ox", 2),
    ("ax", 0),
    ("pass", 5),
    ("early_across",),
    ("ax", 1),
    ("pass", 6),
    ("pass", 7),
    ("ax", 2),
    ("relay", 4),
    ("grad", 3),
    ("ox", 3),
    ("own", 5),
    ("own", 6),
    ("own", 7),
    ("out", 0),
    ("relay", 5),
    ("grad", 4),
    ("ax", 3),
    ("ys", 0),
    ("ox", 4),
    ("relay", 6),
    ("relay", 7),
    ("ay", 0),
    ("grad", 5),
    ("ax", 4),
    ("ox", 5),
    ("grad", 6),
    ("grad", 7),
    ("ox", 6),
    ("ox", 7),
    ("se", 0),
    ("bwd", 0),
    ("ax", 5),
    ("bwd", 1),
    ("ax", 6),
    ("ax", 7),
    ("ys", 1),
    ("far", 0),
    ("ay", 1),
    ("se", 1),
    ("a",),
    ("ac", 0),
    ("far", 1),
    ("b",),
    ("out", 1),
    ("ac", 1),
    ("c",),
    ("fin",),
)


def head_scalars(ref, first, tokens):
    row = lax.broadcasted_iota(jnp.int32, (8, tokens), 0)
    out = jnp.zeros((8, tokens), jnp.float32)
    for r in range(8):
        out = jnp.where(row == r, ref[first + r], out)
    return out


def dot(a, b, over, **settings):
    return lax.dot_general(
        a, b, ((over[:1], over[1:]), ((), ())), preferred_element_type=jnp.float32, **settings
    )


def decays(dt, a_log, dt_bias, first):
    tokens = dt.shape[1]
    raw = dt[...] + head_scalars(dt_bias, first, tokens)
    step = jnp.maximum(raw, 0.0) + jnp.log1p(jnp.exp(-jnp.abs(raw)))
    rate = -jnp.exp(head_scalars(a_log, first, tokens)) * step
    below = lax.broadcasted_iota(jnp.int32, (SPAN, SPAN), 0) >= lax.broadcasted_iota(
        jnp.int32, (SPAN, SPAN), 1
    )
    ones = jnp.where(below, 1.0, 0.0)
    steps, by_row, by_column = [], [], []
    for k in range(2):
        own = rate[:, k * SPAN : (k + 1) * SPAN]
        steps.append(step[:, k * SPAN : (k + 1) * SPAN])
        by_row.append(dot(own, ones, (1, 1), precision=lax.Precision.HIGHEST))
        by_column.append(dot(ones, own, (1, 1), precision=lax.Precision.HIGHEST))
    return below, steps, by_row, by_column


def tail_keys(keys, step, cum):
    weight = jnp.exp(cum[:, SPAN - 1 :] - cum) * step
    turned = keys.astype(jnp.float32).T
    return [(turned * weight[r : r + 1]).astype(jnp.bfloat16) for r in range(8)]


def paired(low, one, two):
    return jnp.where(low, one, two)


def forward_group(
    g, a_log, dt_bias, skip, x_all, z_all, b_all, c_all, dt_all, gain_all, normed, gated_all, tables
):
    first = g * 8
    wide, narrow = slice(g * 512, g * 512 + 512), slice(g * STATE, g * STATE + STATE)
    x_ref, z_ref = x_all.at[:, wide], z_all.at[:, wide]
    b_ref, c_ref = b_all.at[:, narrow], c_all.at[:, narrow]
    dt_ref = dt_all.at[first : first + 8]
    gain_ref, normed_ref, gated_ref = gain_all.at[:, wide], normed.at[:, wide], gated_all.at[:, wide]
    below, steps, by_row, by_column = decays(dt_ref, a_log, dt_bias, first)
    low = lax.broadcasted_iota(jnp.int32, (1, 128), 1) < HEAD_DIM
    tails = tail_keys(b_ref[:SPAN], steps[0], by_row[0])
    for k in range(2):
        rows = slice(k * SPAN, (k + 1) * SPAN)
        scores = dot(c_ref[rows], b_ref[rows], (1, 1))
        squares = jnp.zeros((SPAN, 1), jnp.float32)
        for q in range(4):
            cols = slice(q * 128, (q + 1) * 128)
            values = x_ref[rows, cols]
            sides = []
            for r in (2 * q, 2 * q + 1):
                gap = by_column[k][:, r : r + 1] - by_row[k][r : r + 1]
                table = jnp.where(below, jnp.exp(gap), 0.0)
                weights = (scores * table * steps[k][r : r + 1]).astype(jnp.bfloat16)
                tables[g, k, r] = weights
                sides.append(dot(weights, values, (1, 0)))
            skips = paired(low, skip[first + 2 * q], skip[first + 2 * q + 1])
            out = paired(low, *sides) + skips * values.astype(jnp.float32)
            if k == 1:
                earlier = x_ref[:SPAN, cols]
                state = paired(low, *[dot(tails[r], earlier, (1, 0)) for r in (2 * q, 2 * q + 1)])
                fade = jnp.exp(
                    paired(low, *[by_column[1][:, r : r + 1] for r in (2 * q, 2 * q + 1)])
                )
                out = out + dot(c_ref[rows], state.astype(jnp.bfloat16), (1, 0)) * fade
            z = z_ref[rows, cols].astype(jnp.float32)
            gated = out * (z / (1.0 + jnp.exp(-z)))
            gated_ref[rows, cols] = gated
            squares = squares + jnp.sum(gated * gated, axis=1, keepdims=True)
        scale = lax.rsqrt(squares * (1.0 / 512) + 1e-05)
        normed_ref[rows] = (gated_ref[rows] * scale * gain_ref[...]).astype(jnp.bfloat16)


def backward_group(
    g, a_log, dt_bias, skip, dn_all, gated_all, z_all, tables, b_all, c_all, dt_all, gain_all, grad
):
    first = g * 8
    wide, narrow = slice(g * 512, g * 512 + 512), slice(g * STATE, g * STATE + STATE)
    dn_ref, gated_ref, z_ref = dn_all.at[:, wide], gated_all.at[:, wide], z_all.at[:, wide]
    b_ref, c_ref, dt_ref = b_all.at[:, narrow], c_all.at[:, narrow], dt_all.at[first : first + 8]
    gain_ref, out_ref = gain_all.at[:, wide], grad.at[:, wide]
    _, steps, by_row, by_column = decays(dt_ref, a_log, dt_bias, first)
    low = lax.broadcasted_iota(jnp.int32, (1, 128), 1) < HEAD_DIM
    tails = tail_keys(b_ref[:SPAN], steps[0], by_row[0])
    states = []
    for k in (1, 0):
        rows = slice(k * SPAN, (k + 1) * SPAN)
        gated = gated_ref[rows]
        pulled = dn_ref[rows] * gain_ref[...]
        mean = jnp.sum(gated * gated, axis=1, keepdims=True) * (1.0 / 512)
        scale = lax.rsqrt(mean + 1e-05)
        along = jnp.sum(gated * pulled, axis=1, keepdims=True) * (1.0 / 512)
        fall = along * scale * scale
        for q in range(4):
            cols = slice(q * 128, (q + 1) * 128)
            z = z_ref[rows, cols].astype(jnp.float32)
            own = dn_ref[rows, cols] * gain_ref[:, cols] - gated_ref[rows, cols] * fall
            ssd = own * scale * (z / (1.0 + jnp.exp(-z)))
            short = ssd.astype(jnp.bfloat16)
            sides = [dot(tables[g, k, r], short, (0, 0)) for r in (2 * q, 2 * q + 1)]
            skips = paired(low, skip[first + 2 * q], skip[first + 2 * q + 1])
            grad = paired(low, *sides) + skips * ssd
            if k == 1:
                fade = jnp.exp(
                    paired(low, *[by_column[1][:, r : r + 1] for r in (2 * q, 2 * q + 1)])
                )
                states.append(
                    dot(c_ref[rows], (ssd * fade).astype(jnp.bfloat16), (0, 0)).astype(
                        jnp.bfloat16
                    )
                )
            else:
                grad = grad + paired(
                    low, *[dot(tails[r], states[q], (0, 0)) for r in (2 * q, 2 * q + 1)]
                )
            out_ref[rows, cols] = grad.astype(jnp.bfloat16)


def step_kernel(
    a_log,
    dt_bias,
    skip,
    x_ref,
    z_ref,
    b_ref,
    c_ref,
    dt_ref,
    gain_ref,
    weight_in,
    target,
    global_own,
    momentum_own,
    grad_x,
    pair,
    share,
    new_global,
    new_momentum,
    weight,
    normed,
    gated,
    tables,
    d_normed,
    full,
    part,
    s_far,
    s_near,
    s_mid,
    r_far,
    r_near,
    r_mid,
    cot,
    fresh,
    r_core,
    s_core,
    r_x,
    s_x,
    r_y,
    s_z,
    r_z,
    whole_global,
    delta,
    sq_a,
    sq_b,
    sq_c,
    weight_sem,
    out_sem,
    z_send,
    z_recv,
    core_send,
    core_recv,
    x_send,
    x_recv,
    y_send,
    y_recv,
    zl_send,
    zl_recv,
    early_send,
    early_recv,
    a_send,
    a_recv,
    b_send,
    b_recv,
    c_send,
    c_recv,
    g_send,
    g_recv,
):
    zl = lax.axis_index("replica_0")
    y = lax.axis_index("replica_1")
    x = lax.axis_index("replica_2")
    c = lax.axis_index("replica_3")
    j = lax.axis_index("tensor")

    def on_z(kz, kj):
        return {"replica_0": lax.rem(zl + kz, 2), "tensor": lax.rem(j + kj, 4)}

    def on_x(kx, kc):
        return {"replica_2": lax.rem(x + kx, 4), "replica_3": lax.rem(c + kc, 2)}

    def on_y(ky):
        return {"replica_1": lax.rem(y + ky, 4)}

    z_peers = [(kz, kj) for kz in range(2) for kj in range(4) if kz + kj]
    x_peers = [(kx, kc) for kx in range(4) for kc in range(2) if kx + kc]
    barrier = pltpu.get_barrier_semaphore()
    for kz, kj in z_peers:
        pl.semaphore_signal(barrier, inc=1, device_id=on_z(kz, kj), device_id_type=MESH)
    for kx, kc in x_peers:
        pl.semaphore_signal(barrier, inc=1, device_id=on_x(kx, kc), device_id_type=MESH)
    for ky in range(1, 4):
        pl.semaphore_signal(barrier, inc=1, device_id=on_y(ky), device_id_type=MESH)
    fetch = pltpu.make_async_copy(weight_in, weight, weight_sem)
    fetch.start()

    def forward(g):
        forward_group(
            *[g, a_log, dt_bias, skip, x_ref, z_ref, b_ref, c_ref, dt_ref, gain_ref],
            *[normed, gated, tables],
        )

    forward(0)
    pl.semaphore_wait(barrier, len(z_peers) + len(x_peers) + 3)

    def remote(src, dst, send_sem, recv_sem, device):
        return pltpu.make_async_remote_copy(
            src_ref=src,
            dst_ref=dst,
            send_sem=send_sem,
            recv_sem=recv_sem,
            device_id=device,
            device_id_type=MESH,
        )

    def way(u):
        return 1 - 2 * (u % 2)

    def shard(step):
        return lax.rem(j + step + 4, 4)

    def z_copy(kind, u):
        d = way(u)
        ahead = {"tensor": shard(d)}
        behind = {"tensor": shard(-d)}
        src, dst, device = {
            "far": lambda: (s_far.at[u], r_far.at[u], behind),
            "near": lambda: (s_near.at[u], r_near.at[u], ahead),
            "mid": lambda: (s_mid.at[u], r_mid.at[u], behind),
            "ahead": lambda: (cot.at[u, j], cot.at[u, j], ahead),
            "behind": lambda: (cot.at[u, j], cot.at[u, j], behind),
            "relay": lambda: (cot.at[u, shard(-d)], cot.at[u, shard(-d)], ahead),
        }[kind]()
        slot = KINDS.index(kind)
        return remote(src, dst, z_send.at[u, slot], z_recv.at[u, slot], device)

    def core_copy(u):
        return remote(
            fresh.at[u, :, 1 - c],
            r_core.at[u],
            core_send.at[u],
            core_recv.at[u],
            {"replica_3": 1 - c},
        )

    def x_copy(u, k):
        there = lax.rem(x + k, 4)
        return remote(
            s_core.at[u, there],
            r_x.at[u, k - 1],
            x_send.at[u, k - 1],
            x_recv.at[u, k - 1],
            {"replica_2": there},
        )

    def y_copy(half, k):
        there = lax.rem(y + k, 4)
        return remote(
            s_x.at[half * 4 + there],
            r_y.at[half, k - 1],
            y_send.at[half, k - 1],
            y_recv.at[half, k - 1],
            {"replica_1": there},
        )

    def rows_of(u):
        return slice(u * FEATURES, (u + 1) * FEATURES)

    def begin(u):
        d = way(u)
        products = lax.dot_general(
            normed[...],
            weight[rows_of(u), :],
            (((1,), (1,)), ((), ())),
            preferred_element_type=jnp.float32,
        )
        part[u] = products.reshape(4, TOKENS, FEATURES)
        s_far[u] = part[u, shard(2)].astype(jnp.bfloat16)
        s_near[u] = part[u, shard(d)].astype(jnp.bfloat16)
        z_copy("far", u).start()
        z_copy("near", u).start()

    def pass_on(u):
        z_copy("far", u).wait_recv()
        s_mid[u] = (r_far[u].astype(jnp.float32) + part[u, shard(-way(u))]).astype(jnp.bfloat16)
        z_copy("mid", u).start()

    def own(u):
        z_copy("near", u).wait_recv()
        z_copy("mid", u).wait_recv()
        total = part[u, j] + r_near[u].astype(jnp.float32) + r_mid[u].astype(jnp.float32)
        cot[u, j] = (total - target[:, rows_of(u)].astype(jnp.float32)).astype(jnp.bfloat16)
        z_copy("ahead", u).start()
        z_copy("behind", u).start()

    def relay(u):
        z_copy("ahead", u).wait_recv()
        z_copy("relay", u).start()

    def gradients(u):
        z_copy("behind", u).wait_recv()
        z_copy("relay", u).wait_recv()
        whole = cot[u].reshape(4 * TOKENS, FEATURES)
        for first in range(0, WIDTH, 512):
            cols = slice(first, first + 512)
            rows = weight[rows_of(u), cols]
            grad = lax.dot_general(
                whole,
                normed[:, cols],
                (((0,), (0,)), ((), ())),
                preferred_element_type=jnp.float32,
            )
            moved = (rows.astype(jnp.float32) - inner_rate * grad).astype(jnp.bfloat16)
            fresh[u, :, :, :, cols] = moved.reshape(4, 2, 32, 512)
            d_normed[:, cols] += jnp.dot(whole, rows, preferred_element_type=jnp.float32)
        core_copy(u).start()

    def over_x(u):
        core_copy(u).wait_recv()
        for i in range(4):
            both = fresh[u, i, c].astype(jnp.float32) + r_core[u, i].astype(jnp.float32)
            s_core[u, i] = both.astype(jnp.bfloat16)
        for k in range(1, 4):
            x_copy(u, k).start()

    def after_x(u):
        total = s_core[u, x].astype(jnp.float32)
        for k in range(1, 4):
            x_copy(u, k).wait_recv()
            total = total + r_x[u, k - 1].astype(jnp.float32)
        s_x[u] = total.astype(jnp.bfloat16)

    def zl_copy(half):
        return remote(s_z.at[half], r_z.at[half], zl_send.at[half], zl_recv.at[half], on_z(1, 0))

    def early_copies():
        base = full.at[0, zl, y, x, c]
        return (
            remote(base, base, early_send.at[0], early_recv.at[0], on_z(1, 0)),
            remote(
                global_own, whole_global.at[zl], early_send.at[1], early_recv.at[1], on_z(1, 0)
            ),
        )

    left, right = pl.ds(0, WIDTH // 2), pl.ds(WIDTH // 2, WIDTH // 2)

    def gather(which, half, index, src, device):
        row = which * 2 + half
        return remote(src, src, g_send.at[row, index], g_recv.at[row, index], device)

    def near_copies(which, half):
        piece = full.at[which, half]
        copies = []
        for k in range(1, 4):
            copies.append(gather(which, half, k - 1, piece.at[y, x, c, :, left], on_y(k)))
            copies.append(gather(which, half, k + 2, piece.at[y, x, c, :, right], on_x(k, 0)))
        return copies

    def far_copies(which, half, k):
        piece = full.at[which, half]
        return (
            gather(which, half, k + 5, piece.at[:, x, c, :, left], on_x(k, 0)),
            gather(which, half, k + 8, piece.at[y, :, c, :, right], on_y(k)),
        )

    def across_copies(which, half, k):
        piece = full.at[which, half]
        from_x, from_y = lax.rem(x + 4 - k, 4), lax.rem(y + 4 - k, 4)
        return (
            gather(which, half, 12 + k, piece.at[:, from_x, c, :, left], on_x(0, 1)),
            gather(which, half, 16 + k, piece.at[from_y, :, c, :, right], on_x(0, 1)),
        )

    def near_start(which, half):
        for copy in near_copies(which, half):
            copy.start()

    def far_start(which, half):
        for copy in near_copies(which, half):
            copy.wait_recv()
        for k in (1, 3, 2):
            for copy in far_copies(which, half, k):
                copy.start()
        for copy in across_copies(which, half, 0):
            copy.start()

    def across_start(which, half):
        for k in (1, 3, 2):
            for arrived, copy in zip(far_copies(which, half, k), across_copies(which, half, k)):
                arrived.wait_recv()
                copy.start()

    def y_start(half):
        for k in range(1, 4):
            y_copy(half, k).start()

    def after_y(half):
        total = s_x[half * 4 + y].astype(jnp.float32)
        for k in range(1, 4):
            y_copy(half, k).wait_recv()
            total = total + r_y[half, k - 1].astype(jnp.float32)
        s_z[half] = total.astype(jnp.bfloat16)
        zl_copy(half).start()

    def settle(half):
        zl_copy(half).wait_recv()
        total = s_z[half].astype(jnp.float32) + r_z[half].astype(jnp.float32)
        change = whole_global[half] - total * (1.0 / 64)
        delta[half] = change
        full[1, half, y, x, c] = change.astype(jnp.bfloat16)
        near_start(1, half)

    def early_near():
        for copy in early_copies():
            copy.wait_recv()
        near_start(0, 0)
        near_start(0, 1)

    def early_far():
        far_start(0, 0)
        far_start(0, 1)

    def early_across():
        across_start(0, 0)
        across_start(0, 1)

    whole_global[zl] = global_own[...]
    base = global_own[...] - (outer_rate * outer_beta * outer_beta) * momentum_own[...]
    full[0, zl, y, x, c] = base.astype(jnp.bfloat16)
    d_normed[...] = jnp.zeros_like(d_normed)
    for copy in early_copies():
        copy.start()
    forward(1)
    fetch.wait()
    def sum_a():
        change = delta[zl]
        squares = jnp.sum((change * change).reshape(4, 8, WIDTH), axis=0)
        folded = squares[:, :128]
        for first in range(128, WIDTH, 128):
            folded = folded + squares[:, first : first + 128]
        sq_a[x, c] = folded
        for copy in a_copies:
            copy.start()

    def sum_b():
        for copy in a_copies:
            copy.wait_recv()
        sq_b[y] = jnp.sum(sq_a[...].reshape(8, 8, 128), axis=0)
        for copy in b_copies:
            copy.start()

    def sum_c():
        for copy in b_copies:
            copy.wait_recv()
        sq_c[zl, j] = jnp.sum(sq_b[...], axis=0)
        for copy in c_copies:
            copy.start()

    def out_copies(index):
        if index == 0:
            return [pltpu.make_async_copy(full.at[0], pair.at[0], out_sem.at[0])]
        half = index - 1
        return [pltpu.make_async_copy(full.at[1, half], pair.at[1, half], out_sem.at[index])]

    def out(index):
        for which, half in (((0, 0), (0, 1)) if index == 0 else ((1, index - 1),)):
            for k in range(4):
                for copy in across_copies(which, half, k):
                    copy.wait_recv()
        for copy in out_copies(index):
            copy.start()

    def finish():
        for copy in c_copies:
            copy.wait_recv()
        square_sum = jnp.sum(jnp.sum(sq_c[...].reshape(8, 8, 128), axis=0), keepdims=True)
        factor = jnp.minimum(1.0, clip_rms / jnp.sqrt(square_sum / ENTRIES + 1e-06))
        clipped = factor * delta[zl]
        moment = outer_beta * momentum_own[...] + clipped
        new_momentum[...] = moment
        new_global[...] = global_own[...] - outer_rate * (clipped + outer_beta * moment)
        share[...] = jnp.broadcast_to(factor * (outer_rate * (1.0 + outer_beta)), share.shape)

    def backward(g):
        backward_group(
            *[g, a_log, dt_bias, skip, d_normed, gated, z_ref, tables],
            *[b_ref, c_ref, dt_ref, gain_ref, grad_x],
        )

    a_copies = [
        remote(sq_a.at[x, c], sq_a.at[x, c], a_send.at[i], a_recv.at[i], on_x(*peer))
        for i, peer in enumerate(x_peers)
    ]
    b_copies = [
        remote(sq_b.at[y], sq_b.at[y], b_send.at[k - 1], b_recv.at[k - 1], on_y(k))
        for k in range(1, 4)
    ]
    c_copies = [
        remote(sq_c.at[zl, j], sq_c.at[zl, j], c_send.at[i], c_recv.at[i], on_z(*peer))
        for i, peer in enumerate(z_peers)
    ]
    actions = {
        "begin": begin,
        "pass": pass_on,
        "own": own,
        "relay": relay,
        "grad": gradients,
        "ox": over_x,
        "ax": after_x,
        "early_near": early_near,
        "early_far": early_far,
        "early_across": early_across,
        "ys": y_start,
        "ay": after_y,
        "se": settle,
        "far": lambda half: far_start(1, half),
        "ac": lambda half: across_start(1, half),
        "a": sum_a,
        "b": sum_b,
        "c": sum_c,
        "fin": finish,
        "bwd": backward,
        "out": out,
    }
    for name, *index in ORDER:
        actions[name](*index)
    out(2)

    for index in range(3):
        for copy in out_copies(index):
            copy.wait()
    for copy in [*a_copies, *b_copies, *c_copies, *early_copies()]:
        copy.wait_send()
    for half in range(2):
        zl_copy(half).wait_send()
        for k in range(1, 4):
            y_copy(half, k).wait_send()
        for which in range(2):
            for copy in near_copies(which, half):
                copy.wait_send()
            for k in range(4):
                for copy in across_copies(which, half, k):
                    copy.wait_send()
                if k:
                    for copy in far_copies(which, half, k):
                        copy.wait_send()

    for u in range(UNITS):
        for kind in KINDS:
            z_copy(kind, u).wait_send()
        core_copy(u).wait_send()
        for k in range(1, 4):
            x_copy(u, k).wait_send()


def apply_kernel(pair, share, grad_in, global_in, momentum_in, grad, weight, new_global, moment):
    grad[...] = grad_in[...]
    new_global[...] = global_in[...]
    moment[...] = momentum_in[...]
    factor = share[0:1, 0:1]

    @pl.loop(0, 8)
    def _(i):
        part = pl.ds(pl.multiple_of(i * 64, 64), 64)
        base = pair[0, part].astype(jnp.float32)
        weight[part] = (base - factor * pair[1, part].astype(jnp.float32)).astype(jnp.bfloat16)


def apply(pair, share, grad_x, new_global, new_momentum):
    slim = pl.BlockSpec((128, WIDTH), lambda i: (i, 0))
    rows = pl.BlockSpec((32, 256), lambda i: (0, i))
    grad, weight, new_global, new_momentum = pl.pallas_call(
        apply_kernel,
        grid=(4,),
        out_shape=(
            jax.ShapeDtypeStruct((512, WIDTH), jnp.bfloat16),
            jax.ShapeDtypeStruct((2048, WIDTH), jnp.bfloat16),
            jax.ShapeDtypeStruct((32, WIDTH), jnp.float32),
            jax.ShapeDtypeStruct((32, WIDTH), jnp.float32),
        ),
        in_specs=[
            pl.BlockSpec((2, 512, WIDTH), lambda i: (0, i, 0)),
            pl.BlockSpec((8, 128), lambda i: (0, 0)),
            *[slim, rows, rows],
        ],
        out_specs=[slim, pl.BlockSpec((512, WIDTH), lambda i: (i, 0)), rows, rows],
        compiler_params=pltpu.CompilerParams(vmem_limit_bytes=67043328),
    )(pair, share, grad_x, new_global, new_momentum)
    return grad, weight, new_global, new_momentum


def step(a_log, dt_bias, skip, x_in, gate_z, b_proj, c_proj, dt, gain, weight, target, *outer):
    half = jnp.bfloat16
    piece = (UNITS, TOKENS, FEATURES)
    dma = pltpu.SemaphoreType.DMA
    vmem = pl.BlockSpec(memory_space=pltpu.VMEM)
    smem = pl.BlockSpec(memory_space=pltpu.SMEM)
    grad_x, pair, share, new_global, new_momentum = pl.pallas_call(
        step_kernel,
        out_shape=(
            jax.ShapeDtypeStruct((512, WIDTH), half),
            jax.ShapeDtypeStruct((2, 2, 4, 4, 2, 32, WIDTH), half),
            jax.ShapeDtypeStruct((8, 128), jnp.float32),
            jax.ShapeDtypeStruct((32, WIDTH), jnp.float32),
            jax.ShapeDtypeStruct((32, WIDTH), jnp.float32),
        ),
        in_specs=[*[smem] * 3, *[vmem] * 6, pl.BlockSpec(memory_space=pl.ANY), *[vmem] * 3],
        out_specs=[vmem, pl.BlockSpec(memory_space=pl.ANY), *[vmem] * 3],
        scratch_shapes=[
            pltpu.VMEM((2048, WIDTH), half),
            pltpu.VMEM((512, WIDTH), half),
            pltpu.VMEM((512, WIDTH), jnp.float32),
            pltpu.VMEM((2, 2, 8, SPAN, SPAN), half),
            pltpu.VMEM((512, WIDTH), jnp.float32),
            pltpu.VMEM((2, 2, 4, 4, 2, 32, WIDTH), half),
            pltpu.VMEM((UNITS, 4, TOKENS, FEATURES), jnp.float32),
            *[pltpu.VMEM(piece, half)] * 6,
            pltpu.VMEM((UNITS, 4, TOKENS, FEATURES), half),
            pltpu.VMEM((UNITS, 4, 2, 32, WIDTH), half),
            pltpu.VMEM((UNITS, 4, 32, WIDTH), half),
            pltpu.VMEM((UNITS, 4, 32, WIDTH), half),
            pltpu.VMEM((UNITS, 3, 32, WIDTH), half),
            pltpu.VMEM((UNITS, 32, WIDTH), half),
            pltpu.VMEM((2, 3, 32, WIDTH), half),
            pltpu.VMEM((2, 32, WIDTH), half),
            pltpu.VMEM((2, 32, WIDTH), half),
            pltpu.VMEM((2, 32, WIDTH), jnp.float32),
            pltpu.VMEM((2, 32, WIDTH), jnp.float32),
            pltpu.VMEM((4, 2, 8, 128), jnp.float32),
            pltpu.VMEM((4, 8, 128), jnp.float32),
            pltpu.VMEM((2, 4, 8, 128), jnp.float32),
            dma,
            dma((3,)),
            *[dma((UNITS, len(KINDS)))] * 2,
            *[dma((UNITS,))] * 2,
            *[dma((UNITS, 3))] * 2,
            *[dma((2, 3))] * 2,
            *[dma((2,))] * 2,
            *[dma((2,))] * 2,
            *[dma((7,))] * 2,
            *[dma((3,))] * 2,
            *[dma((7,))] * 2,
            *[dma((4, 20))] * 2,
        ],
        compiler_params=pltpu.CompilerParams(
            collective_id=0, has_side_effects=True, vmem_limit_bytes=67043328
        ),
    )(a_log, dt_bias, skip, x_in, gate_z, b_proj, c_proj, dt, gain, weight, target, *outer)
    return apply(pair.reshape(2, 2048, WIDTH), share, grad_x, new_global, new_momentum)


def shards(
    x_in,
    gate_z,
    b_proj,
    c_proj,
    dt_raw,
    a_log,
    dt_bias,
    skip_d,
    norm_gain,
    out_weight,
    global_weight,
    momentum,
    target,
):
    return step(
        *[a_log, dt_bias, skip_d, x_in, gate_z, b_proj, c_proj, dt_raw.T],
        *[norm_gain.reshape(1, WIDTH), out_weight[0], target, global_weight, momentum],
    )


def solution(mesh):
    torus = Mesh(
        mesh.devices.reshape(2, 4, 4, 2, mesh.shape["tensor"]),
        ("replica_0", "replica_1", "replica_2", "replica_3", "tensor"),
    )
    in_specs = (
        P(REPLICA, "tensor"),
        P(REPLICA, "tensor"),
        P(REPLICA, "tensor"),
        P(REPLICA, "tensor"),
        P(REPLICA, "tensor"),
        P("tensor"),
        P("tensor"),
        P("tensor"),
        P("tensor"),
        P(REPLICA, None, "tensor"),
        P(REPLICA, "tensor"),
        P(REPLICA, "tensor"),
        P(REPLICA_TENSOR, None),
    )
    out_specs = (
        P(REPLICA, "tensor"),
        P(None, "tensor"),
        P(REPLICA, "tensor"),
        P(REPLICA, "tensor"),
    )
    return jax.shard_map(
        shards, mesh=torus, in_specs=in_specs, out_specs=out_specs, check_vma=False
    )
```

```python
import jax
import jax.numpy as jnp
from jax import lax
from jax.experimental import pallas as pl
from jax.experimental.pallas import tpu as pltpu
from jax.sharding import Mesh
from jax.sharding import PartitionSpec as P

HEAD_DIM = 64
STATE = 128
SPAN = 256
REPLICA = ("replica_0", "replica_1", "replica_2", "replica_3")
REPLICA_TENSOR = ("replica_0", "replica_1", "replica_2", "replica_3", "tensor")


inner_rate = 0.001
outer_rate = 0.7
outer_beta = 0.9
clip_rms = 0.005
MESH = pl.DeviceIdType.MESH
UNITS = 8
FEATURES = 256
TOKENS = 128
WIDTH = 1024
ENTRIES = 2048 * 4096
KINDS = ("far", "near", "mid", "ahead", "behind", "relay")
ORDER = (
    ("begin", 0),
    ("begin", 1),
    ("begin", 2),
    ("pass", 0),
    ("early_near",),
    ("pass", 1),
    ("begin", 3),
    ("pass", 2),
    ("begin", 4),
    ("own", 0),
    ("own", 1),
    ("pass", 3),
    ("early_far",),
    ("own", 2),
    ("pass", 4),
    ("relay", 0),
    ("relay", 1),
    ("own", 3),
    ("relay", 2),
    ("grad", 0),
    ("begin", 5),
    ("begin", 6),
    ("ox", 0),
    ("grad", 1),
    ("begin", 7),
    ("relay", 3),
    ("ox", 1),
    ("grad", 2),
    ("early_across",),
    ("pass", 5),
    ("ox", 2),
    ("own", 4),
    ("ax", 0),
    ("pass", 6),
    ("ax", 1),
    ("pass", 7),
    ("ax", 2),
    ("grad", 3),
    ("own", 5),
    ("relay", 4),
    ("ox", 3),
    ("own", 6),
    ("own", 7),
    ("out", 0),
    ("relay", 5),
    ("ax", 3),
    ("ys", 0),
    ("grad", 4),
    ("relay", 6),
    ("relay", 7),
    ("ox", 4),
    ("ay", 0),
    ("grad", 5),
    ("ox", 5),
    ("grad", 6),
    ("grad", 7),
    ("ox", 6),
    ("ox", 7),
    ("se", 0),
    ("ax", 4),
    ("bwd", 1),
    ("ax", 5),
    ("bwd", 0),
    ("ax", 6),
    ("ax", 7),
    ("ys", 1),
    ("far", 0),
    ("ay", 1),
    ("se", 1),
    ("a",),
    ("ac", 0),
    ("b",),
    ("far", 1),
    ("out", 1),
    ("c",),
    ("ac", 1),
    ("fin",),
)


def head_scalars(ref, first, tokens):
    row = lax.broadcasted_iota(jnp.int32, (8, tokens), 0)
    out = jnp.zeros((8, tokens), jnp.float32)
    for r in range(8):
        out = jnp.where(row == r, ref[first + r], out)
    return out


def dot(a, b, over, **settings):
    return lax.dot_general(
        a, b, ((over[:1], over[1:]), ((), ())), preferred_element_type=jnp.float32, **settings
    )


def decays(dt, a_log, dt_bias, first):
    tokens = dt.shape[1]
    raw = dt[...] + head_scalars(dt_bias, first, tokens)
    step = jnp.maximum(raw, 0.0) + jnp.log1p(jnp.exp(-jnp.abs(raw)))
    rate = -jnp.exp(head_scalars(a_log, first, tokens)) * step
    below = lax.broadcasted_iota(jnp.int32, (SPAN, SPAN), 0) >= lax.broadcasted_iota(
        jnp.int32, (SPAN, SPAN), 1
    )
    ones = jnp.where(below, 1.0, 0.0)
    steps, by_row, by_column = [], [], []
    for k in range(2):
        own = rate[:, k * SPAN : (k + 1) * SPAN]
        steps.append(step[:, k * SPAN : (k + 1) * SPAN])
        by_row.append(dot(own, ones, (1, 1), precision=lax.Precision.HIGHEST))
        by_column.append(dot(ones, own, (1, 1), precision=lax.Precision.HIGHEST))
    return below, steps, by_row, by_column


def tail_keys(keys, step, cum):
    weight = jnp.exp(cum[:, SPAN - 1 :] - cum) * step
    turned = keys.astype(jnp.float32).T
    return [(turned * weight[r : r + 1]).astype(jnp.bfloat16) for r in range(8)]


def paired(low, one, two):
    return jnp.where(low, one, two)


def forward_group(
    g, a_log, dt_bias, skip, x_all, z_all, b_all, c_all, dt_all, gain_all, normed, gated_all, tables
):
    first = g * 8
    wide, narrow = slice(g * 512, g * 512 + 512), slice(g * STATE, g * STATE + STATE)
    x_ref, z_ref = x_all.at[:, wide], z_all.at[:, wide]
    b_ref, c_ref = b_all.at[:, narrow], c_all.at[:, narrow]
    dt_ref = dt_all.at[first : first + 8]
    gain_ref, normed_ref, gated_ref = gain_all.at[:, wide], normed.at[:, wide], gated_all.at[:, wide]
    below, steps, by_row, by_column = decays(dt_ref, a_log, dt_bias, first)
    low = lax.broadcasted_iota(jnp.int32, (1, 128), 1) < HEAD_DIM
    tails = tail_keys(b_ref[:SPAN], steps[0], by_row[0])
    corner = below[: SPAN // 2, : SPAN // 2]
    for k in range(2):
        rows = slice(k * SPAN, (k + 1) * SPAN)
        scores = dot(c_ref[rows], b_ref[rows], (1, 1))
        squares = jnp.zeros((SPAN, 1), jnp.float32)
        for q in range(4):
            cols = slice(q * 128, (q + 1) * 128)
            values = x_ref[rows, cols]
            sides = []
            for r in (2 * q, 2 * q + 1):
                late, early = by_column[k][:, r : r + 1], by_row[k][r : r + 1]
                step = steps[k][r : r + 1]
                for top in (0, SPAN // 2):
                    own = slice(top, top + SPAN // 2)
                    table = jnp.where(corner, jnp.exp(late[own] - early[:, own]), 0.0)
                    weights = scores[own, own] * table * step[:, own]
                    tables[g, k, r, own, own] = weights.astype(jnp.bfloat16)
                lower, upper = slice(SPAN // 2, SPAN), slice(0, SPAN // 2)
                table = jnp.exp(late[lower] - early[:, upper])
                weights = scores[lower, upper] * table * step[:, upper]
                tables[g, k, r, lower, upper] = weights.astype(jnp.bfloat16)
                tables[g, k, r, upper, lower] = jnp.zeros((SPAN // 2, SPAN // 2), jnp.bfloat16)
                sides.append(dot(tables[g, k, r], values, (1, 0)))
            skips = paired(low, skip[first + 2 * q], skip[first + 2 * q + 1])
            out = paired(low, *sides) + skips * values.astype(jnp.float32)
            if k == 1:
                earlier = x_ref[:SPAN, cols]
                state = paired(low, *[dot(tails[r], earlier, (1, 0)) for r in (2 * q, 2 * q + 1)])
                fade = jnp.exp(
                    paired(low, *[by_column[1][:, r : r + 1] for r in (2 * q, 2 * q + 1)])
                )
                out = out + dot(c_ref[rows], state.astype(jnp.bfloat16), (1, 0)) * fade
            z = z_ref[rows, cols].astype(jnp.float32)
            gated = out * (z / (1.0 + jnp.exp(-z)))
            gated_ref[rows, cols] = gated
            squares = squares + jnp.sum(gated * gated, axis=1, keepdims=True)
        scale = lax.rsqrt(squares * (1.0 / 512) + 1e-05)
        normed_ref[rows] = (gated_ref[rows] * scale * gain_ref[...]).astype(jnp.bfloat16)


def backward_group(
    g, a_log, dt_bias, skip, dn_all, gated_all, z_all, tables, b_all, c_all, dt_all, gain_all, grad
):
    first = g * 8
    wide, narrow = slice(g * 512, g * 512 + 512), slice(g * STATE, g * STATE + STATE)
    dn_ref, gated_ref, z_ref = dn_all.at[:, wide], gated_all.at[:, wide], z_all.at[:, wide]
    b_ref, c_ref, dt_ref = b_all.at[:, narrow], c_all.at[:, narrow], dt_all.at[first : first + 8]
    gain_ref, out_ref = gain_all.at[:, wide], grad.at[:, wide]
    _, steps, by_row, by_column = decays(dt_ref, a_log, dt_bias, first)
    low = lax.broadcasted_iota(jnp.int32, (1, 128), 1) < HEAD_DIM
    tails = tail_keys(b_ref[:SPAN], steps[0], by_row[0])
    states = []
    for k in (1, 0):
        rows = slice(k * SPAN, (k + 1) * SPAN)
        gated = gated_ref[rows]
        pulled = dn_ref[rows] * gain_ref[...]
        mean = jnp.sum(gated * gated, axis=1, keepdims=True) * (1.0 / 512)
        scale = lax.rsqrt(mean + 1e-05)
        along = jnp.sum(gated * pulled, axis=1, keepdims=True) * (1.0 / 512)
        fall = along * scale * scale
        for q in range(4):
            cols = slice(q * 128, (q + 1) * 128)
            z = z_ref[rows, cols].astype(jnp.float32)
            own = dn_ref[rows, cols] * gain_ref[:, cols] - gated_ref[rows, cols] * fall
            ssd = own * scale * (z / (1.0 + jnp.exp(-z)))
            short = ssd.astype(jnp.bfloat16)
            sides = [dot(tables[g, k, r], short, (0, 0)) for r in (2 * q, 2 * q + 1)]
            skips = paired(low, skip[first + 2 * q], skip[first + 2 * q + 1])
            grad = paired(low, *sides) + skips * ssd
            if k == 1:
                fade = jnp.exp(
                    paired(low, *[by_column[1][:, r : r + 1] for r in (2 * q, 2 * q + 1)])
                )
                states.append(
                    dot(c_ref[rows], (ssd * fade).astype(jnp.bfloat16), (0, 0)).astype(
                        jnp.bfloat16
                    )
                )
            else:
                grad = grad + paired(
                    low, *[dot(tails[r], states[q], (0, 0)) for r in (2 * q, 2 * q + 1)]
                )
            out_ref[rows, cols] = grad.astype(jnp.bfloat16)


def step_kernel(
    a_log,
    dt_bias,
    skip,
    x_ref,
    z_ref,
    b_ref,
    c_ref,
    dt_ref,
    gain_ref,
    weight_in,
    target,
    global_own,
    momentum_own,
    grad_x,
    pair,
    share,
    new_global,
    new_momentum,
    weight,
    normed,
    gated,
    tables,
    d_normed,
    full,
    part,
    s_far,
    s_near,
    s_mid,
    r_far,
    r_near,
    r_mid,
    cot,
    fresh,
    r_core,
    s_core,
    r_x,
    s_x,
    r_y,
    s_z,
    r_z,
    whole_global,
    delta,
    sq_a,
    sq_b,
    sq_c,
    weight_sem,
    out_sem,
    z_send,
    z_recv,
    core_send,
    core_recv,
    x_send,
    x_recv,
    y_send,
    y_recv,
    zl_send,
    zl_recv,
    early_send,
    early_recv,
    a_send,
    a_recv,
    b_send,
    b_recv,
    c_send,
    c_recv,
    g_send,
    g_recv,
):
    zl = lax.axis_index("replica_0")
    y = lax.axis_index("replica_1")
    x = lax.axis_index("replica_2")
    c = lax.axis_index("replica_3")
    j = lax.axis_index("tensor")

    def on_z(kz, kj):
        return {"replica_0": lax.rem(zl + kz, 2), "tensor": lax.rem(j + kj, 4)}

    def on_x(kx, kc):
        return {"replica_2": lax.rem(x + kx, 4), "replica_3": lax.rem(c + kc, 2)}

    def on_y(ky):
        return {"replica_1": lax.rem(y + ky, 4)}

    z_peers = [(kz, kj) for kz in range(2) for kj in range(4) if kz + kj]
    x_peers = [(kx, kc) for kx in range(4) for kc in range(2) if kx + kc]
    barrier = pltpu.get_barrier_semaphore()
    for kz, kj in z_peers:
        pl.semaphore_signal(barrier, inc=1, device_id=on_z(kz, kj), device_id_type=MESH)
    for kx, kc in x_peers:
        pl.semaphore_signal(barrier, inc=1, device_id=on_x(kx, kc), device_id_type=MESH)
    for ky in range(1, 4):
        pl.semaphore_signal(barrier, inc=1, device_id=on_y(ky), device_id_type=MESH)
    fetch = pltpu.make_async_copy(weight_in, weight, weight_sem)
    fetch.start()

    def forward(g):
        forward_group(
            *[g, a_log, dt_bias, skip, x_ref, z_ref, b_ref, c_ref, dt_ref, gain_ref],
            *[normed, gated, tables],
        )

    forward(0)
    pl.semaphore_wait(barrier, len(z_peers) + len(x_peers) + 3)

    def remote(src, dst, send_sem, recv_sem, device):
        return pltpu.make_async_remote_copy(
            src_ref=src,
            dst_ref=dst,
            send_sem=send_sem,
            recv_sem=recv_sem,
            device_id=device,
            device_id_type=MESH,
        )

    def way(u):
        return 1 - 2 * (u % 2)

    def shard(step):
        return lax.rem(j + step + 4, 4)

    def z_copy(kind, u):
        d = way(u)
        ahead = {"tensor": shard(d)}
        behind = {"tensor": shard(-d)}
        src, dst, device = {
            "far": lambda: (s_far.at[u], r_far.at[u], behind),
            "near": lambda: (s_near.at[u], r_near.at[u], ahead),
            "mid": lambda: (s_mid.at[u], r_mid.at[u], behind),
            "ahead": lambda: (cot.at[u, j], cot.at[u, j], ahead),
            "behind": lambda: (cot.at[u, j], cot.at[u, j], behind),
            "relay": lambda: (cot.at[u, shard(-d)], cot.at[u, shard(-d)], ahead),
        }[kind]()
        slot = KINDS.index(kind)
        return remote(src, dst, z_send.at[u, slot], z_recv.at[u, slot], device)

    def core_copy(u):
        return remote(
            fresh.at[u, :, 1 - c],
            r_core.at[u],
            core_send.at[u],
            core_recv.at[u],
            {"replica_3": 1 - c},
        )

    def x_copy(u, k):
        there = lax.rem(x + k, 4)
        return remote(
            s_core.at[u, there],
            r_x.at[u, k - 1],
            x_send.at[u, k - 1],
            x_recv.at[u, k - 1],
            {"replica_2": there},
        )

    def y_copy(half, k):
        there = lax.rem(y + k, 4)
        return remote(
            s_x.at[half * 4 + there],
            r_y.at[half, k - 1],
            y_send.at[half, k - 1],
            y_recv.at[half, k - 1],
            {"replica_1": there},
        )

    def rows_of(u):
        return slice(u * FEATURES, (u + 1) * FEATURES)

    def begin(u):
        d = way(u)
        products = lax.dot_general(
            normed[...],
            weight[rows_of(u), :],
            (((1,), (1,)), ((), ())),
            preferred_element_type=jnp.float32,
        )
        part[u] = products.reshape(4, TOKENS, FEATURES)
        s_far[u] = part[u, shard(2)].astype(jnp.bfloat16)
        s_near[u] = part[u, shard(d)].astype(jnp.bfloat16)
        z_copy("far", u).start()
        z_copy("near", u).start()

    def pass_on(u):
        z_copy("far", u).wait_recv()
        s_mid[u] = (r_far[u].astype(jnp.float32) + part[u, shard(-way(u))]).astype(jnp.bfloat16)
        z_copy("mid", u).start()

    def own(u):
        z_copy("near", u).wait_recv()
        z_copy("mid", u).wait_recv()
        total = part[u, j] + r_near[u].astype(jnp.float32) + r_mid[u].astype(jnp.float32)
        cot[u, j] = (total - target[:, rows_of(u)].astype(jnp.float32)).astype(jnp.bfloat16)
        z_copy("ahead", u).start()
        z_copy("behind", u).start()

    def relay(u):
        z_copy("ahead", u).wait_recv()
        z_copy("relay", u).start()

    def gradients(u):
        z_copy("behind", u).wait_recv()
        z_copy("relay", u).wait_recv()
        whole = cot[u].reshape(4 * TOKENS, FEATURES)
        for first in range(0, WIDTH, 512):
            cols = slice(first, first + 512)
            grad = lax.dot_general(
                whole,
                normed[:, cols],
                (((0,), (0,)), ((), ())),
                preferred_element_type=jnp.float32,
            )
            rows = weight[rows_of(u), cols].astype(jnp.float32)
            moved = (rows - inner_rate * grad).astype(jnp.bfloat16)
            fresh[u, :, :, :, cols] = moved.reshape(4, 2, 32, 512)
        core_copy(u).start()
        for first in range(0, WIDTH, 512):
            cols = slice(first, first + 512)
            d_normed[:, cols] += jnp.dot(
                whole, weight[rows_of(u), cols], preferred_element_type=jnp.float32
            )

    def over_x(u):
        core_copy(u).wait_recv()
        for k in (2, 1, 3, 0):
            i = lax.rem(x + k, 4)
            both = fresh[u, i, c].astype(jnp.float32) + r_core[u, i].astype(jnp.float32)
            s_core[u, i] = both.astype(jnp.bfloat16)
            if k:
                x_copy(u, k).start()

    def after_x(u):
        total = s_core[u, x].astype(jnp.float32)
        for k in range(1, 4):
            x_copy(u, k).wait_recv()
            total = total + r_x[u, k - 1].astype(jnp.float32)
        s_x[u] = total.astype(jnp.bfloat16)

    def zl_copy(half):
        return remote(s_z.at[half], r_z.at[half], zl_send.at[half], zl_recv.at[half], on_z(1, 0))

    def early_copies():
        base = full.at[0, zl, y, x, c]
        return (
            remote(base, base, early_send.at[0], early_recv.at[0], on_z(1, 0)),
            remote(
                global_own, whole_global.at[zl], early_send.at[1], early_recv.at[1], on_z(1, 0)
            ),
        )

    left, right = pl.ds(0, WIDTH // 2), pl.ds(WIDTH // 2, WIDTH // 2)

    def gather(which, half, index, src, device):
        row = which * 2 + half
        return remote(src, src, g_send.at[row, index], g_recv.at[row, index], device)

    def near_copies(which, half):
        piece = full.at[which, half]
        copies = []
        for k in range(1, 4):
            copies.append(gather(which, half, k - 1, piece.at[y, x, c, :, left], on_y(k)))
            copies.append(gather(which, half, k + 2, piece.at[y, x, c, :, right], on_x(k, 0)))
        return copies

    def far_copies(which, half, k):
        piece = full.at[which, half]
        return (
            gather(which, half, k + 5, piece.at[:, x, c, :, left], on_x(k, 0)),
            gather(which, half, k + 8, piece.at[y, :, c, :, right], on_y(k)),
        )

    def across_copies(which, half, k):
        piece = full.at[which, half]
        from_x, from_y = lax.rem(x + 4 - k, 4), lax.rem(y + 4 - k, 4)
        return (
            gather(which, half, 12 + k, piece.at[:, from_x, c, :, left], on_x(0, 1)),
            gather(which, half, 16 + k, piece.at[from_y, :, c, :, right], on_x(0, 1)),
        )

    def near_start(which, half):
        for copy in near_copies(which, half):
            copy.start()

    def far_start(which, half):
        for copy in near_copies(which, half):
            copy.wait_recv()
        for k in (1, 3, 2):
            for copy in far_copies(which, half, k):
                copy.start()
        for copy in across_copies(which, half, 0):
            copy.start()

    def across_start(which, half):
        for k in (1, 3, 2):
            for arrived, copy in zip(far_copies(which, half, k), across_copies(which, half, k)):
                arrived.wait_recv()
                copy.start()

    def y_start(half):
        for k in range(1, 4):
            y_copy(half, k).start()

    def after_y(half):
        total = s_x[half * 4 + y].astype(jnp.float32)
        for k in range(1, 4):
            y_copy(half, k).wait_recv()
            total = total + r_y[half, k - 1].astype(jnp.float32)
        s_z[half] = total.astype(jnp.bfloat16)
        zl_copy(half).start()

    def settle(half):
        zl_copy(half).wait_recv()
        total = s_z[half].astype(jnp.float32) + r_z[half].astype(jnp.float32)
        change = whole_global[half] - total * (1.0 / 64)
        delta[half] = change
        full[1, half, y, x, c] = change.astype(jnp.bfloat16)
        near_start(1, half)

    def early_near():
        for copy in early_copies():
            copy.wait_recv()
        near_start(0, 0)
        near_start(0, 1)

    def early_far():
        far_start(0, 0)
        far_start(0, 1)

    def early_across():
        across_start(0, 0)
        across_start(0, 1)

    whole_global[zl] = global_own[...]
    base = global_own[...] - (outer_rate * outer_beta * outer_beta) * momentum_own[...]
    full[0, zl, y, x, c] = base.astype(jnp.bfloat16)
    d_normed[...] = jnp.zeros_like(d_normed)
    for copy in early_copies():
        copy.start()
    forward(1)
    fetch.wait()
    def sum_a():
        change = delta[zl]
        squares = jnp.sum((change * change).reshape(4, 8, WIDTH), axis=0)
        folded = squares[:, :128]
        for first in range(128, WIDTH, 128):
            folded = folded + squares[:, first : first + 128]
        sq_a[x, c] = folded
        for copy in a_copies:
            copy.start()

    def sum_b():
        for copy in a_copies:
            copy.wait_recv()
        sq_b[y] = jnp.sum(sq_a[...].reshape(8, 8, 128), axis=0)
        for copy in b_copies:
            copy.start()

    def sum_c():
        for copy in b_copies:
            copy.wait_recv()
        sq_c[zl, j] = jnp.sum(sq_b[...], axis=0)
        for copy in c_copies:
            copy.start()

    def out_copies(index):
        if index == 0:
            return [pltpu.make_async_copy(full.at[0], pair.at[0], out_sem.at[0])]
        half = index - 1
        return [pltpu.make_async_copy(full.at[1, half], pair.at[1, half], out_sem.at[index])]

    def out(index):
        for which, half in (((0, 0), (0, 1)) if index == 0 else ((1, index - 1),)):
            for k in range(4):
                for copy in across_copies(which, half, k):
                    copy.wait_recv()
        for copy in out_copies(index):
            copy.start()

    def finish():
        for copy in c_copies:
            copy.wait_recv()
        square_sum = jnp.sum(jnp.sum(sq_c[...].reshape(8, 8, 128), axis=0), keepdims=True)
        factor = jnp.minimum(1.0, clip_rms / jnp.sqrt(square_sum / ENTRIES + 1e-06))
        clipped = factor * delta[zl]
        moment = outer_beta * momentum_own[...] + clipped
        new_momentum[...] = moment
        new_global[...] = global_own[...] - outer_rate * (clipped + outer_beta * moment)
        share[...] = jnp.broadcast_to(factor * (outer_rate * (1.0 + outer_beta)), share.shape)

    def backward(g):
        backward_group(
            *[g, a_log, dt_bias, skip, d_normed, gated, z_ref, tables],
            *[b_ref, c_ref, dt_ref, gain_ref, grad_x],
        )

    a_copies = [
        remote(sq_a.at[x, c], sq_a.at[x, c], a_send.at[i], a_recv.at[i], on_x(*peer))
        for i, peer in enumerate(x_peers)
    ]
    b_copies = [
        remote(sq_b.at[y], sq_b.at[y], b_send.at[k - 1], b_recv.at[k - 1], on_y(k))
        for k in range(1, 4)
    ]
    c_copies = [
        remote(sq_c.at[zl, j], sq_c.at[zl, j], c_send.at[i], c_recv.at[i], on_z(*peer))
        for i, peer in enumerate(z_peers)
    ]
    actions = {
        "begin": begin,
        "pass": pass_on,
        "own": own,
        "relay": relay,
        "grad": gradients,
        "ox": over_x,
        "ax": after_x,
        "early_near": early_near,
        "early_far": early_far,
        "early_across": early_across,
        "ys": y_start,
        "ay": after_y,
        "se": settle,
        "far": lambda half: far_start(1, half),
        "ac": lambda half: across_start(1, half),
        "a": sum_a,
        "b": sum_b,
        "c": sum_c,
        "fin": finish,
        "bwd": backward,
        "out": out,
    }
    for name, *index in ORDER:
        actions[name](*index)
    out(2)

    for index in range(3):
        for copy in out_copies(index):
            copy.wait()
    for copy in [*a_copies, *b_copies, *c_copies, *early_copies()]:
        copy.wait_send()
    for half in range(2):
        zl_copy(half).wait_send()
        for k in range(1, 4):
            y_copy(half, k).wait_send()
        for which in range(2):
            for copy in near_copies(which, half):
                copy.wait_send()
            for k in range(4):
                for copy in across_copies(which, half, k):
                    copy.wait_send()
                if k:
                    for copy in far_copies(which, half, k):
                        copy.wait_send()

    for u in range(UNITS):
        for kind in KINDS:
            z_copy(kind, u).wait_send()
        core_copy(u).wait_send()
        for k in range(1, 4):
            x_copy(u, k).wait_send()


def apply_kernel(pair, share, grad_in, global_in, momentum_in, grad, weight, new_global, moment):
    grad[...] = grad_in[...]
    new_global[...] = global_in[...]
    moment[...] = momentum_in[...]
    factor = share[0:1, 0:1]

    @pl.loop(0, 16)
    def _(i):
        part = pl.ds(pl.multiple_of(i * 64, 64), 64)
        base = pair[0, part].astype(jnp.float32)
        weight[part] = (base - factor * pair[1, part].astype(jnp.float32)).astype(jnp.bfloat16)


def apply(pair, share, grad_x, new_global, new_momentum):
    slim = pl.BlockSpec((256, WIDTH), lambda i: (i, 0))
    rows = pl.BlockSpec((32, 512), lambda i: (0, i))
    grad, weight, new_global, new_momentum = pl.pallas_call(
        apply_kernel,
        grid=(2,),
        out_shape=(
            jax.ShapeDtypeStruct((512, WIDTH), jnp.bfloat16),
            jax.ShapeDtypeStruct((2048, WIDTH), jnp.bfloat16),
            jax.ShapeDtypeStruct((32, WIDTH), jnp.float32),
            jax.ShapeDtypeStruct((32, WIDTH), jnp.float32),
        ),
        in_specs=[
            pl.BlockSpec((2, 1024, WIDTH), lambda i: (0, i, 0)),
            pl.BlockSpec((8, 128), lambda i: (0, 0)),
            *[slim, rows, rows],
        ],
        out_specs=[slim, pl.BlockSpec((1024, WIDTH), lambda i: (i, 0)), rows, rows],
        compiler_params=pltpu.CompilerParams(vmem_limit_bytes=67043328),
    )(pair, share, grad_x, new_global, new_momentum)
    return grad, weight, new_global, new_momentum


def step(a_log, dt_bias, skip, x_in, gate_z, b_proj, c_proj, dt, gain, weight, target, *outer):
    half = jnp.bfloat16
    piece = (UNITS, TOKENS, FEATURES)
    dma = pltpu.SemaphoreType.DMA
    vmem = pl.BlockSpec(memory_space=pltpu.VMEM)
    smem = pl.BlockSpec(memory_space=pltpu.SMEM)
    grad_x, pair, share, new_global, new_momentum = pl.pallas_call(
        step_kernel,
        out_shape=(
            jax.ShapeDtypeStruct((512, WIDTH), half),
            jax.ShapeDtypeStruct((2, 2, 4, 4, 2, 32, WIDTH), half),
            jax.ShapeDtypeStruct((8, 128), jnp.float32),
            jax.ShapeDtypeStruct((32, WIDTH), jnp.float32),
            jax.ShapeDtypeStruct((32, WIDTH), jnp.float32),
        ),
        in_specs=[*[smem] * 3, *[vmem] * 6, pl.BlockSpec(memory_space=pl.ANY), *[vmem] * 3],
        out_specs=[vmem, pl.BlockSpec(memory_space=pl.ANY), *[vmem] * 3],
        scratch_shapes=[
            pltpu.VMEM((2048, WIDTH), half),
            pltpu.VMEM((512, WIDTH), half),
            pltpu.VMEM((512, WIDTH), jnp.float32),
            pltpu.VMEM((2, 2, 8, SPAN, SPAN), half),
            pltpu.VMEM((512, WIDTH), jnp.float32),
            pltpu.VMEM((2, 2, 4, 4, 2, 32, WIDTH), half),
            pltpu.VMEM((UNITS, 4, TOKENS, FEATURES), jnp.float32),
            *[pltpu.VMEM(piece, half)] * 6,
            pltpu.VMEM((UNITS, 4, TOKENS, FEATURES), half),
            pltpu.VMEM((UNITS, 4, 2, 32, WIDTH), half),
            pltpu.VMEM((UNITS, 4, 32, WIDTH), half),
            pltpu.VMEM((UNITS, 4, 32, WIDTH), half),
            pltpu.VMEM((UNITS, 3, 32, WIDTH), half),
            pltpu.VMEM((UNITS, 32, WIDTH), half),
            pltpu.VMEM((2, 3, 32, WIDTH), half),
            pltpu.VMEM((2, 32, WIDTH), half),
            pltpu.VMEM((2, 32, WIDTH), half),
            pltpu.VMEM((2, 32, WIDTH), jnp.float32),
            pltpu.VMEM((2, 32, WIDTH), jnp.float32),
            pltpu.VMEM((4, 2, 8, 128), jnp.float32),
            pltpu.VMEM((4, 8, 128), jnp.float32),
            pltpu.VMEM((2, 4, 8, 128), jnp.float32),
            dma,
            dma((3,)),
            *[dma((UNITS, len(KINDS)))] * 2,
            *[dma((UNITS,))] * 2,
            *[dma((UNITS, 3))] * 2,
            *[dma((2, 3))] * 2,
            *[dma((2,))] * 2,
            *[dma((2,))] * 2,
            *[dma((7,))] * 2,
            *[dma((3,))] * 2,
            *[dma((7,))] * 2,
            *[dma((4, 20))] * 2,
        ],
        compiler_params=pltpu.CompilerParams(
            collective_id=0, has_side_effects=True, vmem_limit_bytes=67043328
        ),
    )(a_log, dt_bias, skip, x_in, gate_z, b_proj, c_proj, dt, gain, weight, target, *outer)
    return apply(pair.reshape(2, 2048, WIDTH), share, grad_x, new_global, new_momentum)


def shards(
    x_in,
    gate_z,
    b_proj,
    c_proj,
    dt_raw,
    a_log,
    dt_bias,
    skip_d,
    norm_gain,
    out_weight,
    global_weight,
    momentum,
    target,
):
    return step(
        *[a_log, dt_bias, skip_d, x_in, gate_z, b_proj, c_proj, dt_raw.T],
        *[norm_gain.reshape(1, WIDTH), out_weight[0], target, global_weight, momentum],
    )


def solution(mesh):
    torus = Mesh(
        mesh.devices.reshape(2, 4, 4, 2, mesh.shape["tensor"]),
        ("replica_0", "replica_1", "replica_2", "replica_3", "tensor"),
    )
    in_specs = (
        P(REPLICA, "tensor"),
        P(REPLICA, "tensor"),
        P(REPLICA, "tensor"),
        P(REPLICA, "tensor"),
        P(REPLICA, "tensor"),
        P("tensor"),
        P("tensor"),
        P("tensor"),
        P("tensor"),
        P(REPLICA, None, "tensor"),
        P(REPLICA, "tensor"),
        P(REPLICA, "tensor"),
        P(REPLICA_TENSOR, None),
    )
    out_specs = (
        P(REPLICA, "tensor"),
        P(None, "tensor"),
        P(REPLICA, "tensor"),
        P(REPLICA, "tensor"),
    )
    return jax.shard_map(
        shards, mesh=torus, in_specs=in_specs, out_specs=out_specs, check_vma=False
    )
```
